512 devices in a mesh: grp: 8 (over y, core), own: 64 (over z, x).
Axes of the slice: x: 4, y: 4, z: 16, core: 2. Of those that a mesh axis runs over, the one named last changes fastest.
Arguments:
- amplitudes: bfloat16 [3072, 128, 128], P('own', 'grp'), may hold values from -6 to 6
- integrals: bfloat16 [49152, 8192], P('own', 'grp'), may hold values from -0.02734375 to 0.02734375
- tile_block: int32 [3072], P('own'), may hold values from 0 to 7, as said below
- tile_index: int32 [3072], P('own'), may hold values from 0 to 383, as said below
Outputs:
- ladder: float32 [1024, 8192], P('own', 'grp')
The draws below stay inside these ranges and needn't reach their ends.
Inputs may be any that keep to these rules, and one draw needn't show every extreme that they name: Each pair (tile_block, tile_index) is named by at most one of the 3072 tile rows. Of the 48 rows of one own index, at most 2 have tile_index in one owner's range o * 6 to (o + 1) * 6 - 1, and exactly 2 do for some owners. Exactly 48 of all tile rows have tile_index in each owner's range. `tile_index`: owner o holds integral rows of tiles o * 6 to (o + 1) * 6 - 1.
All inputs are finite; a program needn't handle non-finite values.
Results may differ from the reference program's by a relative error of at most 0.0003.
Values may be sent and summed in bfloat16 or wider, within the bound.
No kernel may reach another device: no remote copies, remote signals or barrier semaphores. Data moves between devices by JAX's collectives and lax.ppermute only.
A program may use at most 64 MiB of HBM per device.

```python
import jax
import jax.numpy as jnp
from jax import lax

TS = 128
TILE_DEV = 6
NB = 8
OCC = 128
ROWS_DEV = 48
ROWS = 3072
CD = 49152
AB = 8192


def tile_plan(key):
    source_count = ROWS // ROWS_DEV
    keys_owner = NB * TILE_DEV
    eighth = source_count // 8
    key_pattern, key_rotate, key_owner, key_shuffle = jax.random.split(jax.random.fold_in(key, 7), 4)
    owner_pos = jnp.arange(source_count)
    pattern = jnp.where(owner_pos < 2 * eighth, 2, jnp.where(owner_pos < 4 * eighth, 1, 0)).astype(jnp.int32)
    pattern = jax.random.permutation(key_pattern, pattern)
    rotation = jax.random.permutation(key_rotate, source_count).astype(jnp.int32)
    counts = pattern[(owner_pos[None, :] - rotation[:, None]) % source_count]
    offsets = jnp.cumsum(counts, axis=0) - counts
    owner_perm = jax.vmap(lambda k: jax.random.permutation(k, keys_owner))(jax.random.split(key_owner, source_count)).astype(jnp.int32)

    def one_source(c, o, k):
        cum_ends = jnp.cumsum(c)
        j = jnp.arange(ROWS_DEV)
        row_owner = jnp.searchsorted(cum_ends, j, side='right').astype(jnp.int32)
        within_rank = j - (cum_ends[row_owner] - c[row_owner])
        key_slot = o[row_owner] + within_rank
        key_values = owner_perm[row_owner, key_slot]
        shuffle = jax.random.permutation(k, ROWS_DEV)
        return (row_owner[shuffle], key_values[shuffle])
    owners, key_values = jax.vmap(one_source)(counts, offsets, jax.random.split(key_shuffle, source_count))
    row_block = (key_values // TILE_DEV).astype(jnp.int32)
    row_tile = (owners * TILE_DEV + key_values % TILE_DEV).astype(jnp.int32)
    return (row_block.reshape(-1), row_tile.reshape(-1))


def draw_tile_block(key, part):
    return tile_plan(key)[0]


def draw_tile_index(key, part):
    return tile_plan(key)[1]


def levels(key, dims, shards, smallest, top_value):
    def one(axis_at, shards_of):
        steps = jax.random.uniform(jax.random.fold_in(jax.random.fold_in(key, 6), axis_at), (shards_of,), jnp.float32, smallest / len(shards), top_value / len(shards))
        return jnp.repeat(jnp.exp(steps), dims[axis_at] // shards_of).reshape((-1,) + (1,) * (len(dims) - axis_at - 1))

    factor_of = one(*shards[0])
    for cut in shards[1:]:
        factor_of = factor_of * one(*cut)
    return factor_of


def gaussian(rng, dims, deviation, most, cuts=(), dtype=jnp.bfloat16):
    gain = levels(rng, dims, cuts, -0.22, 0.18) if cuts else 1.0
    drawn = jax.random.normal(rng, dims, jnp.float32) * deviation * gain
    return jnp.minimum(jnp.maximum(drawn, -most), most).astype(dtype)


def setup_inputs(seed: int = 0) -> dict:
    streams_of = jax.random.split(jax.random.key(seed), 5)
    return {
        "amplitudes": gaussian(streams_of[0], (ROWS, OCC, TS), 1.0, 6.0, ((0, 64), (1, 8))),
        "integrals": gaussian(streams_of[1], (CD, AB), (ROWS * TS // NB) ** -0.5, 0.02734375, ((0, 64), (1, 8))),
        "tile_block": draw_tile_block(jax.random.fold_in(streams_of[4], 71), 0),
        "tile_index": draw_tile_index(jax.random.fold_in(streams_of[4], 71), 0),
    }


def reference(amplitudes, integrals, tile_block, tile_index):
    occ_rows = amplitudes.shape[1]
    tile_width = amplitudes.shape[2]
    totals = jnp.zeros((NB * occ_rows, integrals.shape[1]), jnp.float32)

    def add_tile(running, scanned):
        amp_tile, row_block, row_tile = scanned
        columns = lax.dynamic_slice_in_dim(integrals, (row_tile * tile_width).astype(jnp.int32), tile_width, 0)
        product = jnp.dot(amp_tile, columns, preferred_element_type=jnp.float32)
        row_start = (row_block * occ_rows).astype(jnp.int32)
        current = lax.dynamic_slice_in_dim(running, row_start, occ_rows, 0)
        return lax.dynamic_update_slice_in_dim(running, current + product, row_start, 0), None

    ladder, _ = lax.scan(add_tile, totals, (amplitudes, tile_block, tile_index))
    return ladder
```

```python
import jax
import jax.numpy as jnp
from jax import lax
from jax.experimental import pallas as pl
from jax.experimental.pallas import tpu as pltpu
from jax.sharding import PartitionSpec as P

NB = 8
CAP = 2
NX = 4
TOP = 32767.0
STEPS = 64.0
TINY = 1e-30
VMEM = pl.BlockSpec(memory_space=pltpu.VMEM)
SMEM = pl.BlockSpec(memory_space=pltpu.SMEM)
PARAMS = pltpu.CompilerParams(vmem_limit_bytes=40 << 20)


def code_of(largest):
    return jnp.ceil(jnp.log2(jnp.maximum(largest, TINY)) * STEPS)


def coded(values, code):
    scaled = values * (jnp.exp2(code * (-1.0 / STEPS)) * (TOP - 1.0))
    return jnp.round(scaled).astype(jnp.int32).astype(jnp.int16)


def scale_of(code16):
    code = code16.astype(jnp.int32).astype(jnp.float32)
    return jnp.exp2(code * (1.0 / STEPS)) * (1.0 / (TOP - 1.0))


def plain(values16):
    return values16.astype(jnp.int32).astype(jnp.float32)


def pack(tile_dev, nz, amp, block, index, out, keys, count):
    rows = amp.shape[0]
    owners = nz * NX

    def clear(o, _):
        count[o] = 0
        return 0

    lax.fori_loop(0, owners, clear, 0)
    keys[...] = jnp.full(keys.shape, -1.0, jnp.float32)
    for r in range(rows):
        tile = index[r]
        owner = tile // tile_dev
        rank = count[owner]
        count[owner] = rank + 1
        key = block[r] * tile_dev + (tile - owner * tile_dev)
        z = owner // NX
        x = owner - z * NX
        slot = z * CAP + rank
        out[x, slot] = amp[r]
        keys[x, pl.ds(slot, 1), :] = jnp.full((1, keys.shape[2]), key, jnp.int32).astype(jnp.float32)
    slots = nz * CAP
    occ = amp.shape[1]
    for x in range(NX):
        for part in range(slots // occ):
            out[x, slots + part] = keys[x, part * occ : (part + 1) * occ, :].astype(out.dtype)


def repack(nz, got, out, keys):
    occ = got.shape[2]
    slots = nz * CAP
    for x in range(NX):
        for part in range(slots // occ):
            keys[x, part * occ : (part + 1) * occ, :] = got[x, slots + part].astype(jnp.float32)
    for z in range(nz):
        for x in range(NX):
            for s in range(CAP):
                out[z, x * CAP + s] = got[x, z * CAP + s]
    width = NX * CAP
    for z in range(nz):
        lines = [keys[x, z * CAP : (z + 1) * CAP, :] for x in range(NX)]
        lines += [jnp.full((occ - width, keys.shape[2]), -1.0, jnp.float32)]
        out[z, width] = jnp.concatenate(lines, axis=0).astype(out.dtype)


def place(tile_dev, got, out, held, row, key, sem):
    nz, _, occ, width = got.shape
    per = NX * CAP
    count = nz * per
    marks = jnp.concatenate([got[z, per].astype(jnp.float32)[:per] for z in range(nz)], axis=0)
    at = lax.broadcasted_iota(jnp.int32, (count, width), 0)
    of = lax.broadcasted_iota(jnp.int32, (count, width), 1)
    line = jnp.sum(jnp.where(at == of, marks, 0.0), axis=0, keepdims=True)
    row[...] = line.astype(jnp.int32)
    copy = pltpu.make_async_copy(row, key, sem)
    copy.start()
    copy.wait()
    spare = NB * tile_dev
    for z in range(nz):
        for s in range(per):
            k = key[0, z * per + s]
            held[jnp.where(k < 0, spare, k)] = got[z, s]
    for b in range(NB):
        for t in range(tile_dev):
            out[b * occ : (b + 1) * occ, t * width : (t + 1) * width] = held[b * tile_dev + t]


def multiply(a, v, out):
    rows, cols = a.shape[1], v.shape[1]
    parts = a.shape[0] // NX
    for x in range(NX):
        for h in range(parts):
            p = jnp.dot(a[x + NX * h], v[...], preferred_element_type=jnp.float32)
            grouped = p.reshape(rows // 8, 8, cols)
            code = code_of(jnp.max(jnp.abs(grouped), axis=0))
            q = coded(grouped, code[None])
            out[x, h * rows : (h + 1) * rows, :] = q.reshape(rows, cols)
            out[x, parts * rows + 8 * h : parts * rows + 8 * (h + 1), :] = code.astype(jnp.int32).astype(jnp.int16)


def add_x(rows, got, out):
    parts = (got.shape[1] - 16) // rows
    cols = got.shape[2]
    occ = rows // NB
    tiles = cols // 128
    for h in range(parts):
        total = None
        for x in range(NX):
            scale = scale_of(got[x, parts * rows + 8 * h : parts * rows + 8 * (h + 1), :])
            term = plain(got[x, h * rows : (h + 1) * rows, :]).reshape(rows // 8, 8, cols) * scale[None]
            total = term if total is None else total + term
        total = total.reshape(rows, cols)
        for b in range(NB):
            chunk = total[b * occ : (b + 1) * occ]
            lanes = [chunk[:, 128 * t : 128 * (t + 1)] for t in range(tiles)]
            largest = jnp.abs(lanes[0])
            for lane in lanes[1:]:
                largest = jnp.maximum(largest, jnp.abs(lane))
            code = code_of(largest)
            z = parts * b + h
            for t in range(tiles):
                out[z, t * occ : (t + 1) * occ, :] = coded(lanes[t], code)
            out[z, tiles * occ : (tiles + 1) * occ, :] = code.astype(jnp.int32).astype(jnp.int16)


def add_z(got, out):
    nz = got.shape[0]
    occ = out.shape[0]
    tiles = out.shape[1] // 128
    scales = [scale_of(got[z, tiles * occ : (tiles + 1) * occ, :]) for z in range(nz)]
    for t in range(tiles):
        total = None
        for z in range(nz):
            term = plain(got[z, t * occ : (t + 1) * occ, :]) * scales[z]
            total = term if total is None else total + term
        out[:, 128 * t : 128 * (t + 1)] = total


def call(body, out, ins, scratch=()):
    return pl.pallas_call(
        body, out_shape=out, in_specs=ins, out_specs=VMEM, scratch_shapes=list(scratch), compiler_params=PARAMS
    )


def local(amplitudes, integrals, tile_block, tile_index):
    own = lax.axis_size("own")
    nz = own // NX
    x_groups = [[z * NX + x for x in range(NX)] for z in range(nz)]
    z_groups = [[z * NX + x for z in range(nz)] for x in range(NX)]

    def exchange(array, groups):
        return lax.all_to_all(array, "own", 0, 0, axis_index_groups=groups, tiled=True)

    _, occ, width = amplitudes.shape
    tile_dev = integrals.shape[0] // width
    cols = integrals.shape[1]
    slots = nz * CAP
    dtype = amplitudes.dtype
    struct = jax.ShapeDtypeStruct

    packed = call(
        lambda *refs: pack(tile_dev, nz, *refs),
        struct((NX, slots + slots // occ, occ, width), dtype),
        [VMEM, SMEM, SMEM],
        [pltpu.VMEM((NX, slots, width), jnp.float32), pltpu.SMEM((own,), jnp.int32)],
    )(amplitudes, tile_block, tile_index)
    got = exchange(packed, x_groups)
    turned = call(
        lambda *refs: repack(nz, *refs),
        struct((nz, NX * CAP + 1, occ, width), dtype),
        [VMEM],
        [pltpu.VMEM((NX, slots, width), jnp.float32)],
    )(got)
    got = exchange(turned, z_groups)
    mine = call(
        lambda *refs: place(tile_dev, *refs),
        struct((NB * occ, tile_dev * width), dtype),
        [VMEM],
        [
            pltpu.VMEM((NB * tile_dev + 1, occ, width), dtype),
            pltpu.VMEM((1, width), jnp.int32),
            pltpu.SMEM((1, width), jnp.int32),
            pltpu.SemaphoreType.DMA,
        ],
    )(got)
    dense = lax.all_gather(mine, "grp", axis=0)
    rows = NB * occ
    parts = dense.shape[0] // NX
    sent = call(multiply, struct((NX, parts * rows + 8 * parts, cols), jnp.int16), [VMEM, VMEM])(dense, integrals)
    got = exchange(sent, x_groups)
    sent = call(
        lambda *refs: add_x(rows, *refs),
        struct((nz, (cols // 128 + 1) * occ, 128), jnp.int16),
        [VMEM],
    )(got)
    got = exchange(sent, z_groups)
    return call(add_z, struct((occ, cols), jnp.float32), [VMEM])(got)


def solution(mesh):
    return jax.shard_map(
        local,
        mesh=mesh,
        in_specs=(P("own", "grp", None), P("own", "grp"), P("own"), P("own")),
        out_specs=P("own", "grp"),
        check_vma=False,
    )
```

```python
import jax
import jax.numpy as jnp
from jax import lax
from jax.experimental import pallas as pl
from jax.experimental.pallas import tpu as pltpu
from jax.sharding import PartitionSpec as P

NB = 8
CAP = 2
NX = 4
CHUNKS = 2
CORES = 2
LOWS = 4
TOP = 32767.0
STEPS = 64.0
TINY = 1e-30
VMEM = pl.BlockSpec(memory_space=pltpu.VMEM)
SMEM = pl.BlockSpec(memory_space=pltpu.SMEM)
PARAMS = pltpu.CompilerParams(vmem_limit_bytes=40 << 20)


def code_of(largest):
    return jnp.ceil(jnp.log2(jnp.maximum(largest, TINY)) * STEPS)


def coded(values, code):
    scaled = values * (jnp.exp2(code * (-1.0 / STEPS)) * (TOP - 1.0))
    return jnp.round(scaled).astype(jnp.int32).astype(jnp.int16)


def scale_of(code16):
    code = code16.astype(jnp.int32).astype(jnp.float32)
    return jnp.exp2(code * (1.0 / STEPS)) * (1.0 / (TOP - 1.0))


def plain(values16):
    return values16.astype(jnp.int32).astype(jnp.float32)


def pack(tile_dev, amp, block, index, *refs):
    outs, (keys, count) = refs[:CHUNKS], refs[CHUNKS:]
    owners, lines, lanes = keys.shape

    def clear(o, _):
        count[o] = 0
        return 0

    lax.fori_loop(0, owners, clear, 0)
    keys[...] = jnp.full(keys.shape, -1.0, jnp.float32)
    occ = outs[0].shape[2]
    for r in range(amp.shape[0]):
        tile = index[r]
        owner = tile // tile_dev
        rank = count[owner]
        count[owner] = rank + 1
        key = block[r] * tile_dev + (tile - owner * tile_dev)
        for c, out in enumerate(outs):
            out[owner, rank] = amp[r, c * occ : (c + 1) * occ, :]
        keys[owner, pl.ds(rank, 1), :] = jnp.full((1, lanes), key, jnp.int32).astype(jnp.float32)
    for o in range(owners):
        outs[0][o, CAP] = keys[o].astype(outs[0].dtype)


def place(tile_dev, first, got, out, held, row, key, sem):
    sources, _, occ, width = got.shape
    line = lax.broadcasted_iota(jnp.int32, (occ, width), 0)
    lane = lax.broadcasted_iota(jnp.int32, (occ, width), 1)
    slot = jnp.where(line < CAP, lane - line, -1)
    marks = jnp.zeros((occ, width), jnp.float32)
    for s in range(sources):
        marks = jnp.where(slot == CAP * s, first[s, CAP].astype(jnp.float32), marks)
    row[...] = jnp.sum(marks, axis=0, keepdims=True).astype(jnp.int32)
    copy = pltpu.make_async_copy(row, key, sem)
    copy.start()
    copy.wait()
    spare = NB * tile_dev
    for s in range(sources):
        for r in range(CAP):
            k = key[0, s * CAP + r]
            held[jnp.where(k < 0, spare, k)] = got[s, r]
    for b in range(NB):
        for t in range(tile_dev):
            tile = held[b * tile_dev + t]
            for y in range(out.shape[0]):
                out[y, b * occ : (b + 1) * occ, t * width : (t + 1) * width] = tile


def multiply(mine, theirs, v, core, out):
    rows, cols = mine.shape[1], v.shape[1]
    parts = mine.shape[0] * CORES // NX
    for other, a in enumerate((mine, theirs)):
        c = core[0] if other == 0 else 1 - core[0]
        for even in range(NX // CORES):
            x = even * CORES + c
            sums = [
                jnp.dot(a[even + h * (NX // CORES)], v[...], preferred_element_type=jnp.float32)
                .reshape(rows // 8, 8, cols)
                for h in range(parts)
            ]
            code = None
            for p in sums:
                largest = jnp.max(jnp.abs(p), axis=0)
                code = largest if code is None else jnp.maximum(code, largest)
            code = code_of(code)
            for h, p in enumerate(sums):
                out[x, h * rows : (h + 1) * rows, :] = coded(p, code[None]).reshape(rows, cols)
            out[x, parts * rows : parts * rows + 8, :] = code.astype(jnp.int32).astype(jnp.int16)


def recoded(tiles, out, z):
    largest = jnp.abs(tiles[0])
    for tile in tiles[1:]:
        largest = jnp.maximum(largest, jnp.abs(tile))
    code = code_of(largest)
    lines = code.shape[0]
    for t, tile in enumerate([*tiles, None]):
        out[z, t * lines : (t + 1) * lines, :] = (
            code.astype(jnp.int32).astype(jnp.int16) if tile is None else coded(tile, code)
        )


def decoded(got, lines):
    sources, count = got.shape[0], got.shape[1] // lines - 1
    scales = [scale_of(got[s, count * lines :, :]) for s in range(sources)]
    tiles = []
    for t in range(count):
        total = None
        for s in range(sources):
            term = plain(got[s, t * lines : (t + 1) * lines, :]) * scales[s]
            total = term if total is None else total + term
        tiles.append(total)
    return tiles


def add_x(rows, got, out):
    parts = (got.shape[1] - 8) // rows
    cols = got.shape[2]
    occ = rows // NB
    lows = out.shape[0]
    scales = [scale_of(got[x, parts * rows : parts * rows + 8, :]) for x in range(NX)]
    tiles = [[] for _ in range(lows)]
    for b in range(NB):
        for h in range(parts):
            total = None
            at = h * rows + b * occ
            for x in range(NX):
                term = plain(got[x, at : at + occ, :]) * scales[x]
                total = term if total is None else total + term
            z = parts * b + h
            tiles[z % lows] += [total[:, 128 * t : 128 * (t + 1)] for t in range(cols // 128)]
    for low in range(lows):
        recoded(tiles[low], out, low)


def add_low(occ, got, out):
    tiles = decoded(got, occ)
    count = len(tiles) // out.shape[0]
    for high in range(out.shape[0]):
        recoded(tiles[high * count : (high + 1) * count], out, high)


def add_high(*refs):
    *gots, out = refs
    occ = out.shape[0] // len(gots)
    for c, got in enumerate(gots):
        for t, tile in enumerate(decoded(got, occ)):
            out[c * occ : (c + 1) * occ, 128 * t : 128 * (t + 1)] = tile


def call(body, out, ins, scratch=()):
    specs = [VMEM] * len(out) if isinstance(out, list) else VMEM
    return pl.pallas_call(
        body, out_shape=out, in_specs=ins, out_specs=specs, scratch_shapes=list(scratch), compiler_params=PARAMS
    )


def local(amplitudes, integrals, tile_block, tile_index):
    own, grp = lax.axis_size("own"), lax.axis_size("grp")
    nz, ny = own // NX, grp // CORES
    highs = nz // LOWS
    x_groups = [[z * NX + x for x in range(NX)] for z in range(nz)]
    low_groups = [[(high * LOWS + low) * NX + x for low in range(LOWS)] for high in range(highs) for x in range(NX)]
    high_groups = [[(high * LOWS + low) * NX + x for high in range(highs)] for low in range(LOWS) for x in range(NX)]
    y_groups = [[y * CORES + c for y in range(ny)] for c in range(CORES)]
    core_pairs = [(y * CORES + c, y * CORES + 1 - c) for y in range(ny) for c in range(CORES)]

    def exchange(array, groups=None, axis="own"):
        return lax.all_to_all(array, axis, 0, 0, axis_index_groups=groups, tiled=True)

    _, occ, width = amplitudes.shape
    occ = occ // CHUNKS
    tile_dev = integrals.shape[0] // width
    cols = integrals.shape[1]
    rows = NB * occ
    parts = grp // NX
    tiles = cols // 128
    dtype = amplitudes.dtype
    struct = jax.ShapeDtypeStruct
    core = jnp.reshape(lax.axis_index("grp") % CORES, (1,)).astype(jnp.int32)

    packed = call(
        lambda *refs: pack(tile_dev, *refs),
        [struct((own, CAP + (c == 0), occ, width), dtype) for c in range(CHUNKS)],
        [VMEM, SMEM, SMEM],
        [pltpu.VMEM((own, occ, width), jnp.float32), pltpu.SMEM((own,), jnp.int32)],
    )(amplitudes, tile_block, tile_index)
    moved = [exchange(part) for part in packed]
    sums = []
    for part in moved:
        copies = call(
            lambda *refs: place(tile_dev, *refs),
            struct((ny, rows, tile_dev * width), dtype),
            [VMEM, VMEM],
            [
                pltpu.VMEM((NB * tile_dev + 1, occ, width), dtype),
                pltpu.VMEM((1, width), jnp.int32),
                pltpu.SMEM((1, width), jnp.int32),
                pltpu.SemaphoreType.DMA,
            ],
        )(moved[0], part)
        mine = exchange(copies, y_groups, "grp")
        theirs = lax.ppermute(mine, "grp", core_pairs)
        sent = call(
            multiply, struct((NX, parts * rows + 8, cols), jnp.int16), [VMEM, VMEM, VMEM, SMEM]
        )(mine, theirs, integrals, core)
        sent = call(
            lambda *refs: add_x(rows, *refs), struct((LOWS, (highs * tiles + 1) * occ, 128), jnp.int16), [VMEM]
        )(exchange(sent, x_groups))
        sent = call(
            lambda *refs: add_low(occ, *refs), struct((highs, (tiles + 1) * occ, 128), jnp.int16), [VMEM]
        )(exchange(sent, low_groups))
        sums.append(exchange(sent, high_groups))
    return call(add_high, struct((occ * CHUNKS, cols), jnp.float32), [VMEM] * CHUNKS)(*sums)


def solution(mesh):
    return jax.shard_map(
        local,
        mesh=mesh,
        in_specs=(P("own", "grp", None), P("own", "grp"), P("own"), P("own")),
        out_specs=P("own", "grp"),
        check_vma=False,
    )
```

```python
import jax
import jax.numpy as jnp
from jax import lax
from jax.experimental import pallas as pl
from jax.experimental.pallas import tpu as pltpu
from jax.sharding import PartitionSpec as P

NB = 8
CAP = 2
NX = 4
UNIT = 8
CORES = 2
LOWS = 4
TOP = 32767.0
STEPS = 64.0
TINY = 1e-30
VMEM = pl.BlockSpec(memory_space=pltpu.VMEM)
SMEM = pl.BlockSpec(memory_space=pltpu.SMEM)
PARAMS = pltpu.CompilerParams(vmem_limit_bytes=40 << 20)


def code_of(largest):
    return jnp.ceil(jnp.log2(jnp.maximum(largest, TINY)) * STEPS)


def coded(values, code):
    scaled = values * (jnp.exp2(code * (-1.0 / STEPS)) * (TOP - 1.0))
    return jnp.round(scaled).astype(jnp.int32).astype(jnp.int16)


def scale_of(code16):
    code = code16.astype(jnp.int32).astype(jnp.float32)
    return jnp.exp2(code * (1.0 / STEPS)) * (1.0 / (TOP - 1.0))


def plain(values16):
    return values16.astype(jnp.int32).astype(jnp.float32)


def pack(tile_dev, amp, block, index, out, keys, count):
    owners, _, lanes = keys.shape
    units = amp.shape[1] // UNIT

    def clear(o, _):
        count[o] = 0
        return 0

    lax.fori_loop(0, owners, clear, 0)
    keys[...] = jnp.full(keys.shape, -1.0, jnp.float32)
    for r in range(amp.shape[0]):
        tile = index[r]
        owner = tile // tile_dev
        rank = count[owner]
        count[owner] = rank + 1
        key = block[r] * tile_dev + (tile - owner * tile_dev)
        for u in range(units):
            out[owner, rank * units + u] = amp[r, u * UNIT : (u + 1) * UNIT, :]
        keys[owner, pl.ds(rank, 1), :] = jnp.full((1, lanes), key, jnp.int32).astype(jnp.float32)
    for o in range(owners):
        out[o, CAP * units] = keys[o].astype(out.dtype)


def place(tile_dev, got, out, held, row, key, sem):
    sources, units, _, width = got.shape
    units = (units - 1) // CAP
    line = lax.broadcasted_iota(jnp.int32, (UNIT, width), 0)
    lane = lax.broadcasted_iota(jnp.int32, (UNIT, width), 1)
    slot = jnp.where(line < CAP, lane - line, -1)
    marks = jnp.zeros((UNIT, width), jnp.float32)
    for s in range(sources):
        marks = jnp.where(slot == CAP * s, got[s, CAP * units].astype(jnp.float32), marks)
    row[...] = jnp.sum(marks, axis=0, keepdims=True).astype(jnp.int32)
    copy = pltpu.make_async_copy(row, key, sem)
    copy.start()
    copy.wait()
    spare = NB * tile_dev
    for s in range(sources):
        for r in range(CAP):
            k = key[0, s * CAP + r]
            to = jnp.where(k < 0, spare, k)
            for u in range(units):
                held[to, u] = got[s, r * units + u]
    for b in range(NB):
        for t in range(tile_dev):
            for u in range(units):
                tile = held[b * tile_dev + t, u]
                at = (b * units + u) * UNIT
                for y in range(out.shape[0]):
                    out[y, at : at + UNIT, t * width : (t + 1) * width] = tile


def multiply(a, mine, theirs, which, out):
    rows, cols = a.shape[1], out.shape[1]
    half = NX // CORES

    def block(v):
        sums = [
            jnp.dot(a[which[0] + half * h], v[...], preferred_element_type=jnp.float32).reshape(rows // 8, 8, cols)
            for h in range(a.shape[0] // half)
        ]
        largest = None
        for p in sums:
            top = jnp.max(jnp.abs(p), axis=0)
            largest = top if largest is None else jnp.maximum(largest, top)
        code = code_of(largest)
        for h, p in enumerate(sums):
            out[h * rows : (h + 1) * rows, :] = coded(p, code[None]).reshape(rows, cols)
        out[len(sums) * rows :, :] = code.astype(jnp.int32).astype(jnp.int16)

    @pl.when(which[1] == 0)
    def _():
        block(mine)

    @pl.when(which[1] != 0)
    def _():
        block(theirs)


def recoded(tiles, out, z):
    largest = jnp.abs(tiles[0])
    for tile in tiles[1:]:
        largest = jnp.maximum(largest, jnp.abs(tile))
    code = code_of(largest)
    lines = code.shape[0]
    for t, tile in enumerate([*tiles, None]):
        out[z, t * lines : (t + 1) * lines, :] = (
            code.astype(jnp.int32).astype(jnp.int16) if tile is None else coded(tile, code)
        )


def decoded(got, lines):
    sources, count = got.shape[0], got.shape[1] // lines - 1
    scales = [scale_of(got[s, count * lines :, :]) for s in range(sources)]
    tiles = []
    for t in range(count):
        total = None
        for s in range(sources):
            term = plain(got[s, t * lines : (t + 1) * lines, :]) * scales[s]
            total = term if total is None else total + term
        tiles.append(total)
    return tiles


def add_x(rows, *refs):
    *gots, out = refs
    parts = (gots[0].shape[0] - 8) // rows
    cols = gots[0].shape[1]
    occ = rows // NB
    lows = out.shape[0]
    scales = [scale_of(got[parts * rows :, :]) for got in gots]
    tiles = [[] for _ in range(lows)]
    for b in range(NB):
        for h in range(parts):
            z = parts * b + h
            for u in range(occ // UNIT):
                total = None
                at = h * rows + b * occ + u * UNIT
                for got, scale in zip(gots, scales):
                    term = plain(got[at : at + UNIT, :]) * scale
                    total = term if total is None else total + term
                tiles[z % lows] += [total[:, 128 * t : 128 * (t + 1)] for t in range(cols // 128)]
    for low in range(lows):
        recoded(tiles[low], out, low)


def add_low(got, out):
    tiles = decoded(got, UNIT)
    count = len(tiles) // out.shape[0]
    for high in range(out.shape[0]):
        recoded(tiles[high * count : (high + 1) * count], out, high)


def add_high(got, out):
    lanes = out.shape[1] // 128
    for n, tile in enumerate(decoded(got, UNIT)):
        u, t = n // lanes, n % lanes
        out[u * UNIT : (u + 1) * UNIT, 128 * t : 128 * (t + 1)] = tile


def call(body, out, ins, scratch=()):
    specs = [VMEM] * len(out) if isinstance(out, list) else VMEM
    return pl.pallas_call(
        body, out_shape=out, in_specs=ins, out_specs=specs, scratch_shapes=list(scratch), compiler_params=PARAMS
    )


def local(amplitudes, integrals, tile_block, tile_index):
    own, grp = lax.axis_size("own"), lax.axis_size("grp")
    nz, ny = own // NX, grp // CORES
    highs, half = nz // LOWS, NX // CORES
    low_groups = [[(high * LOWS + low) * NX + x for low in range(LOWS)] for high in range(highs) for x in range(NX)]
    high_groups = [[(high * LOWS + low) * NX + x for high in range(highs)] for low in range(LOWS) for x in range(NX)]
    y_groups = [[y * CORES + c for y in range(ny)] for c in range(CORES)]
    core_pairs = [(y * CORES + c, y * CORES + 1 - c) for y in range(ny) for c in range(CORES)]

    def target(r, x):
        return (r // CORES) ^ (x // CORES), (r % CORES) ^ (x % CORES)

    def round_pairs(r):
        pairs = []
        for g in range(grp):
            for o in range(own):
                y, c, z, x = g // CORES, g % CORES, o // NX, o % NX
                a, to = target(r, x)
                pairs.append((g * own + o, (y * CORES + to) * own + z * NX + a * CORES + c))
        return pairs

    def exchange(array, groups=None, axis="own"):
        return lax.all_to_all(array, axis, 0, 0, axis_index_groups=groups, tiled=True)

    _, occ, width = amplitudes.shape
    units = occ // UNIT
    tile_dev = integrals.shape[0] // width
    cols = integrals.shape[1]
    rows = NB * occ
    parts = grp // NX
    tiles = cols // 128
    dtype = amplitudes.dtype
    struct = jax.ShapeDtypeStruct
    core = lax.axis_index("grp") % CORES
    x = lax.axis_index("own") % NX

    packed = call(
        lambda *refs: pack(tile_dev, *refs),
        struct((own, CAP * units + 1, UNIT, width), dtype),
        [VMEM, SMEM, SMEM],
        [pltpu.VMEM((own, UNIT, width), jnp.float32), pltpu.SMEM((own,), jnp.int32)],
    )(amplitudes, tile_block, tile_index)
    theirs = lax.ppermute(integrals, "grp", core_pairs)
    copies = call(
        lambda *refs: place(tile_dev, *refs),
        struct((ny, rows, tile_dev * width), dtype),
        [VMEM],
        [
            pltpu.VMEM((NB * tile_dev + 1, units, UNIT, width), dtype),
            pltpu.VMEM((1, width), jnp.int32),
            pltpu.SMEM((1, width), jnp.int32),
            pltpu.SemaphoreType.DMA,
        ],
    )(exchange(packed))
    mine = exchange(copies, y_groups, "grp")
    gots = []
    for r in range(half * CORES):
        a, to = target(r, x)
        which = jnp.stack([a, to ^ core]).astype(jnp.int32)
        sent = call(multiply, struct((parts * rows + 8, cols), jnp.int16), [VMEM, VMEM, VMEM, SMEM])(
            mine, integrals, theirs, which
        )
        gots.append(lax.ppermute(sent, ("grp", "own"), round_pairs(r)))
    sent = call(
        lambda *refs: add_x(rows, *refs),
        struct((LOWS, (highs * units * tiles + 1) * UNIT, 128), jnp.int16),
        [VMEM] * len(gots),
    )(*gots)
    sent = call(add_low, struct((highs, (units * tiles + 1) * UNIT, 128), jnp.int16), [VMEM])(
        exchange(sent, low_groups)
    )
    return call(add_high, struct((occ, cols), jnp.float32), [VMEM])(exchange(sent, high_groups))


def solution(mesh):
    return jax.shard_map(
        local,
        mesh=mesh,
        in_specs=(P("own", "grp", None), P("own", "grp"), P("own"), P("own")),
        out_specs=P("own", "grp"),
        check_vma=False,
    )
```

```python
import jax
import jax.numpy as jnp
from jax import lax
from jax.experimental import pallas as pl
from jax.experimental.pallas import tpu as pltpu
from jax.sharding import PartitionSpec as P

NB = 8
CAP = 2
NX = 4
UNIT = 8
CORES = 2
LOWS = 4
TOP = 32767.0
STEPS = 64.0
TINY = 1e-30
VMEM = pl.BlockSpec(memory_space=pltpu.VMEM)
SMEM = pl.BlockSpec(memory_space=pltpu.SMEM)
PARAMS = pltpu.CompilerParams(vmem_limit_bytes=40 << 20)


def code_of(largest):
    return jnp.ceil(jnp.log2(jnp.maximum(largest, TINY)) * STEPS)


def coded(values, code):
    scaled = values * (jnp.exp2(code * (-1.0 / STEPS)) * (TOP - 1.0))
    return jnp.round(scaled).astype(jnp.int32).astype(jnp.int16)


def scale_of(code16):
    code = code16.astype(jnp.int32).astype(jnp.float32)
    return jnp.exp2(code * (1.0 / STEPS)) * (1.0 / (TOP - 1.0))


def plain(values16):
    return values16.astype(jnp.int32).astype(jnp.float32)


def pack(tile_dev, amp, index, out, count):
    owners = out.shape[0]

    def clear(o, _):
        count[o] = 0
        return 0

    lax.fori_loop(0, owners, clear, 0)
    for r in range(amp.shape[0]):
        owner = index[r] // tile_dev
        rank = count[owner]
        count[owner] = rank + 1
        out[owner, rank] = amp[r]


def place(tile_dev, got, key, out, held):
    sources, _, occ, width = got.shape
    spare = NB * tile_dev
    for s in range(sources):
        for r in range(CAP):
            k = key[s * CAP + r]
            held[jnp.where(k < 0, spare, k)] = got[s, r]
    for b in range(NB):
        for t in range(tile_dev):
            tile = held[b * tile_dev + t]
            for y in range(out.shape[0]):
                out[y, b * occ : (b + 1) * occ, t * width : (t + 1) * width] = tile


def slot_keys(plan, first, count):
    key = plan - first
    at = lax.broadcasted_iota(jnp.int32, plan.shape, 1)
    hit = (key >= 0) & (key < count)
    low = jnp.min(jnp.where(hit, at, plan.shape[1]), axis=1, keepdims=True)
    high = jnp.max(jnp.where(hit, at, -1), axis=1, keepdims=True)
    one = jnp.max(jnp.where(hit & (at == low), key, -1), axis=1)
    two = jnp.max(jnp.where(hit & (at == high) & (high > low), key, -1), axis=1)
    return jnp.stack([one, two], axis=1).reshape(-1)


def multiply(a, mine, theirs, which, out):
    rows, cols = a.shape[1], out.shape[1]
    half = NX // CORES

    def block(v):
        sums = [
            jnp.dot(a[which[0] + half * h], v[...], preferred_element_type=jnp.float32).reshape(rows // 8, 8, cols)
            for h in range(a.shape[0] // half)
        ]
        largest = None
        for p in sums:
            top = jnp.max(jnp.abs(p), axis=0)
            largest = top if largest is None else jnp.maximum(largest, top)
        code = code_of(largest)
        for h, p in enumerate(sums):
            out[h * rows : (h + 1) * rows, :] = coded(p, code[None]).reshape(rows, cols)
        out[len(sums) * rows :, :] = code.astype(jnp.int32).astype(jnp.int16)

    @pl.when(which[1] == 0)
    def _():
        block(mine)

    @pl.when(which[1] != 0)
    def _():
        block(theirs)


def recoded(tiles, out):
    largest = jnp.abs(tiles[0])
    for tile in tiles[1:]:
        largest = jnp.maximum(largest, jnp.abs(tile))
    code = code_of(largest)
    lines = code.shape[0]
    for t, tile in enumerate([*tiles, None]):
        out[t * lines : (t + 1) * lines, :] = (
            code.astype(jnp.int32).astype(jnp.int16) if tile is None else coded(tile, code)
        )


def decoded(got, lines):
    sources, count = got.shape[0], got.shape[1] // lines - 1
    scales = [scale_of(got[s, count * lines :, :]) for s in range(sources)]
    tiles = []
    for t in range(count):
        total = None
        for s in range(sources):
            term = plain(got[s, t * lines : (t + 1) * lines, :]) * scales[s]
            total = term if total is None else total + term
        tiles.append(total)
    return tiles


def add_x(rows, *refs):
    *gots, out = refs
    parts = (gots[0].shape[0] - 8) // rows
    cols = gots[0].shape[1]
    occ = rows // NB
    lows = out.shape[0]
    scales = [scale_of(got[parts * rows :, :]) for got in gots]
    tiles = [[] for _ in range(lows)]
    for b in range(NB):
        for h in range(parts):
            z = parts * b + h
            for u in range(occ // UNIT):
                total = None
                at = h * rows + b * occ + u * UNIT
                for got, scale in zip(gots, scales):
                    term = plain(got[at : at + UNIT, :]) * scale
                    total = term if total is None else total + term
                tiles[z % lows] += [total[:, 128 * t : 128 * (t + 1)] for t in range(cols // 128)]
    for low in range(lows):
        recoded(tiles[low], out.at[low])


def add_low(which, got, own, *refs):
    *outs, held = refs
    highs = held.shape[0]
    tiles = decoded(got, UNIT)
    count = len(tiles) // highs
    for n, tile in enumerate(tiles):
        held[n // count, n % count] = tile
    own[...] = held[which[0]]
    for k, out in enumerate(outs):
        high = lax.rem(which[0] + (k + 1), highs)
        recoded([held[high, n] for n in range(count)], out)


def add_high(own, *refs):
    *gots, out = refs
    lanes = out.shape[1] // 128
    count = own.shape[0]
    scales = [scale_of(got[count * UNIT :, :]) for got in gots]
    for n in range(count):
        total = own[n]
        for got, scale in zip(gots, scales):
            total = total + plain(got[n * UNIT : (n + 1) * UNIT, :]) * scale
        u, t = n // lanes, n % lanes
        out[u * UNIT : (u + 1) * UNIT, 128 * t : 128 * (t + 1)] = total


def call(body, out, ins, scratch=()):
    specs = [VMEM] * len(out) if isinstance(out, list) else VMEM
    return pl.pallas_call(
        body, out_shape=out, in_specs=ins, out_specs=specs, scratch_shapes=list(scratch), compiler_params=PARAMS
    )


def local(amplitudes, integrals, tile_block, tile_index):
    own, grp = lax.axis_size("own"), lax.axis_size("grp")
    nz, ny = own // NX, grp // CORES
    highs, half = nz // LOWS, NX // CORES
    low_groups = [[(high * LOWS + low) * NX + x for low in range(LOWS)] for high in range(highs) for x in range(NX)]
    y_groups = [[y * CORES + c for y in range(ny)] for c in range(CORES)]
    core_pairs = [(y * CORES + c, y * CORES + 1 - c) for y in range(ny) for c in range(CORES)]

    def target(r, x):
        return (r // CORES) ^ (x // CORES), (r % CORES) ^ (x % CORES)

    def round_pairs(r):
        pairs = []
        for g in range(grp):
            for o in range(own):
                y, c, z, x = g // CORES, g % CORES, o // NX, o % NX
                a, to = target(r, x)
                pairs.append((g * own + o, (y * CORES + to) * own + z * NX + a * CORES + c))
        return pairs

    def exchange(array, groups=None, axis="own"):
        return lax.all_to_all(array, axis, 0, 0, axis_index_groups=groups, tiled=True)

    _, occ, width = amplitudes.shape
    units = occ // UNIT
    tile_dev = integrals.shape[0] // width
    cols = integrals.shape[1]
    rows = NB * occ
    parts = grp // NX
    tiles = cols // 128
    dtype = amplitudes.dtype
    struct = jax.ShapeDtypeStruct
    core = lax.axis_index("grp") % CORES
    x = lax.axis_index("own") % NX

    def high_pairs(k):
        far = LOWS * NX
        return [(o, (o + k * far) % own) for o in range(own)]

    packed = call(
        lambda *refs: pack(tile_dev, *refs),
        struct((own, CAP, occ, width), dtype),
        [VMEM, SMEM],
        [pltpu.SMEM((own,), jnp.int32)],
    )(amplitudes, tile_index)
    theirs = lax.ppermute(integrals, "grp", core_pairs)
    got = exchange(packed)
    keys = NB * tile_dev
    owner = tile_index // tile_dev
    plan = lax.all_gather(owner * keys + tile_block * tile_dev + (tile_index - owner * tile_dev), "own", axis=0)
    copies = call(
        lambda *refs: place(tile_dev, *refs),
        struct((ny, rows, tile_dev * width), dtype),
        [VMEM, SMEM],
        [pltpu.VMEM((keys + 1, occ, width), dtype)],
    )(got, slot_keys(plan, lax.axis_index("own") * keys, keys))
    mine = exchange(copies, y_groups, "grp")
    gots = []
    for r in (2, 3, 0, 1):
        a, to = target(r, x)
        which = jnp.stack([a, to ^ core]).astype(jnp.int32)
        sent = call(multiply, struct((parts * rows + 8, cols), jnp.int16), [VMEM, VMEM, VMEM, SMEM])(
            mine, integrals, theirs, which
        )
        gots.append(lax.ppermute(sent, ("grp", "own"), round_pairs(r)))
    sent = call(
        lambda *refs: add_x(rows, *refs),
        struct((LOWS, (highs * units * tiles + 1) * UNIT, 128), jnp.int16),
        [VMEM] * len(gots),
    )(*gots)
    count = units * tiles
    part = struct(((count + 1) * UNIT, 128), jnp.int16)
    high = jnp.reshape(lax.axis_index("own") // (LOWS * NX), (1,)).astype(jnp.int32)
    kept, *sent = call(
        add_low,
        [struct((count, UNIT, 128), jnp.float32)] + [part] * (highs - 1),
        [SMEM, VMEM],
        [pltpu.VMEM((highs, count, UNIT, 128), jnp.float32)],
    )(high, exchange(sent, low_groups))
    sent = {k: lax.ppermute(sent[k - 1], "own", high_pairs(k)) for k in (2, 1, 3)}
    return call(add_high, struct((occ, cols), jnp.float32), [VMEM] * highs)(kept, *sent.values())


def solution(mesh):
    return jax.shard_map(
        local,
        mesh=mesh,
        in_specs=(P("own", "grp", None), P("own", "grp"), P("own"), P("own")),
        out_specs=P("own", "grp"),
        check_vma=False,
    )
```

```python
import jax
import jax.numpy as jnp
from jax import lax
from jax.experimental import pallas as pl
from jax.experimental.pallas import tpu as pltpu
from jax.sharding import PartitionSpec as P

NB = 8
CAP = 2
NX = 4
UNIT = 8
CORES = 2
LOWS = 4
TOP = 32767.0
STEPS = 64.0
TINY = 1e-30
VMEM = pl.BlockSpec(memory_space=pltpu.VMEM)
SMEM = pl.BlockSpec(memory_space=pltpu.SMEM)
PARAMS = pltpu.CompilerParams(vmem_limit_bytes=40 << 20)


def code_of(largest):
    return jnp.ceil(jnp.log2(jnp.maximum(largest, TINY)) * STEPS)


def coded(values, code):
    scaled = values * (jnp.exp2(code * (-1.0 / STEPS)) * (TOP - 1.0))
    return jnp.round(scaled).astype(jnp.int32).astype(jnp.int16)


def scale_of(code16):
    code = code16.astype(jnp.int32).astype(jnp.float32)
    return jnp.exp2(code * (1.0 / STEPS)) * (1.0 / (TOP - 1.0))


def plain(values16):
    return values16.astype(jnp.int32).astype(jnp.float32)


def pack(tile_dev, amp, block, index, out, keys, count):
    owners, _, lanes = keys.shape
    units = amp.shape[1] // UNIT

    def clear(o, _):
        count[o] = 0
        return 0

    lax.fori_loop(0, owners, clear, 0)
    keys[...] = jnp.full(keys.shape, -1.0, jnp.float32)
    for r in range(amp.shape[0]):
        tile = index[r]
        owner = tile // tile_dev
        rank = count[owner]
        count[owner] = rank + 1
        key = block[r] * tile_dev + (tile - owner * tile_dev)
        for u in range(units):
            out[owner, rank * units + u] = amp[r, u * UNIT : (u + 1) * UNIT, :]
        keys[owner, pl.ds(rank, 1), :] = jnp.full((1, lanes), key, jnp.int32).astype(jnp.float32)
    for o in range(owners):
        out[o, CAP * units] = keys[o].astype(out.dtype)


def place(tile_dev, got, out, held, row, key, sem):
    sources, units, _, width = got.shape
    units = (units - 1) // CAP
    line = lax.broadcasted_iota(jnp.int32, (UNIT, width), 0)
    lane = lax.broadcasted_iota(jnp.int32, (UNIT, width), 1)
    slot = jnp.where(line < CAP, lane - line, -1)
    marks = jnp.zeros((UNIT, width), jnp.float32)
    for s in range(sources):
        marks = jnp.where(slot == CAP * s, got[s, CAP * units].astype(jnp.float32), marks)
    row[...] = jnp.sum(marks, axis=0, keepdims=True).astype(jnp.int32)
    copy = pltpu.make_async_copy(row, key, sem)
    copy.start()
    copy.wait()
    spare = NB * tile_dev
    for s in range(sources):
        for r in range(CAP):
            k = key[0, s * CAP + r]
            to = jnp.where(k < 0, spare, k)
            for u in range(units):
                held[to, u] = got[s, r * units + u]
    for b in range(NB):
        for t in range(tile_dev):
            for u in range(units):
                tile = held[b * tile_dev + t, u]
                at = (b * units + u) * UNIT
                for y in range(out.shape[0]):
                    out[y, at : at + UNIT, t * width : (t + 1) * width] = tile


def multiply(a, mine, theirs, which, out):
    rows, cols = a.shape[1], out.shape[1]
    half = NX // CORES

    def block(v):
        sums = [
            jnp.dot(a[which[0] + half * h], v[...], preferred_element_type=jnp.float32).reshape(rows // 8, 8, cols)
            for h in range(a.shape[0] // half)
        ]
        largest = None
        for p in sums:
            top = jnp.max(jnp.abs(p), axis=0)
            largest = top if largest is None else jnp.maximum(largest, top)
        code = code_of(largest)
        for h, p in enumerate(sums):
            out[h * rows : (h + 1) * rows, :] = coded(p, code[None]).reshape(rows, cols)
        out[len(sums) * rows :, :] = code.astype(jnp.int32).astype(jnp.int16)

    @pl.when(which[1] == 0)
    def _():
        block(mine)

    @pl.when(which[1] != 0)
    def _():
        block(theirs)


def recoded(tiles, out, z):
    largest = jnp.abs(tiles[0])
    for tile in tiles[1:]:
        largest = jnp.maximum(largest, jnp.abs(tile))
    code = code_of(largest)
    lines = code.shape[0]
    for t, tile in enumerate([*tiles, None]):
        out[z, t * lines : (t + 1) * lines, :] = (
            code.astype(jnp.int32).astype(jnp.int16) if tile is None else coded(tile, code)
        )


def decoded(got, lines):
    sources, count = got.shape[0], got.shape[1] // lines - 1
    scales = [scale_of(got[s, count * lines :, :]) for s in range(sources)]
    tiles = []
    for t in range(count):
        total = None
        for s in range(sources):
            term = plain(got[s, t * lines : (t + 1) * lines, :]) * scales[s]
            total = term if total is None else total + term
        tiles.append(total)
    return tiles


def add_x(rows, *refs):
    *gots, out = refs
    parts = (gots[0].shape[0] - 8) // rows
    cols = gots[0].shape[1]
    occ = rows // NB
    lows = out.shape[0]
    scales = [scale_of(got[parts * rows :, :]) for got in gots]
    tiles = [[] for _ in range(lows)]
    for b in range(NB):
        for h in range(parts):
            z = parts * b + h
            for u in range(occ // UNIT):
                total = None
                at = h * rows + b * occ + u * UNIT
                for got, scale in zip(gots, scales):
                    term = plain(got[at : at + UNIT, :]) * scale
                    total = term if total is None else total + term
                tiles[z % lows] += [total[:, 128 * t : 128 * (t + 1)] for t in range(cols // 128)]
    for low in range(lows):
        recoded(tiles[low], out, low)


def add_low(got, out):
    tiles = decoded(got, UNIT)
    count = len(tiles) // out.shape[0]
    for high in range(out.shape[0]):
        recoded(tiles[high * count : (high + 1) * count], out, high)


def add_high(got, out):
    lanes = out.shape[1] // 128
    for n, tile in enumerate(decoded(got, UNIT)):
        u, t = n // lanes, n % lanes
        out[u * UNIT : (u + 1) * UNIT, 128 * t : 128 * (t + 1)] = tile


def call(body, out, ins, scratch=()):
    specs = [VMEM] * len(out) if isinstance(out, list) else VMEM
    return pl.pallas_call(
        body, out_shape=out, in_specs=ins, out_specs=specs, scratch_shapes=list(scratch), compiler_params=PARAMS
    )


def local(amplitudes, integrals, tile_block, tile_index):
    own, grp = lax.axis_size("own"), lax.axis_size("grp")
    nz, ny = own // NX, grp // CORES
    highs = nz // LOWS
    low_groups = []
    for g in range(grp):
        shift = g % CORES * (LOWS // CORES)
        for high in range(highs):
            line = sorted(((high * LOWS + low + shift) % nz for low in range(LOWS)), key=lambda z: z % LOWS)
            low_groups += [[g * own + z * NX + x for z in line] for x in range(NX)]
    high_groups = [[(high * LOWS + low) * NX + x for high in range(highs)] for low in range(LOWS) for x in range(NX)]
    y_groups = [[y * CORES + c for y in range(ny)] for c in range(CORES)]
    core_pairs = [(y * CORES + c, y * CORES + 1 - c) for y in range(ny) for c in range(CORES)]

    def target(r, x):
        return (r // CORES) ^ (x // CORES), (r % CORES) ^ (x % CORES)

    def round_pairs(r):
        pairs = []
        for g in range(grp):
            for o in range(own):
                y, c, z, x = g // CORES, g % CORES, o // NX, o % NX
                a, to = target(r, x)
                pairs.append((g * own + o, (y * CORES + to) * own + z * NX + a * CORES + c))
        return pairs

    def exchange(array, groups=None, axis="own"):
        return lax.all_to_all(array, axis, 0, 0, axis_index_groups=groups, tiled=True)

    _, occ, width = amplitudes.shape
    units = occ // UNIT
    tile_dev = integrals.shape[0] // width
    cols = integrals.shape[1]
    rows = NB * occ
    parts = grp // NX
    tiles = cols // 128
    dtype = amplitudes.dtype
    struct = jax.ShapeDtypeStruct
    core = lax.axis_index("grp") % CORES
    x = lax.axis_index("own") % NX

    packed = call(
        lambda *refs: pack(tile_dev, *refs),
        struct((own, CAP * units + 1, UNIT, width), dtype),
        [VMEM, SMEM, SMEM],
        [pltpu.VMEM((own, UNIT, width), jnp.float32), pltpu.SMEM((own,), jnp.int32)],
    )(amplitudes, tile_block, tile_index)
    theirs = lax.ppermute(integrals, "grp", core_pairs)
    copies = call(
        lambda *refs: place(tile_dev, *refs),
        struct((ny, rows, tile_dev * width), dtype),
        [VMEM],
        [
            pltpu.VMEM((NB * tile_dev + 1, units, UNIT, width), dtype),
            pltpu.VMEM((1, width), jnp.int32),
            pltpu.SMEM((1, width), jnp.int32),
            pltpu.SemaphoreType.DMA,
        ],
    )(exchange(packed))
    mine = exchange(copies, y_groups, "grp")
    gots = []
    for r in (2, 3, 0, 1):
        a, to = target(r, x)
        which = jnp.stack([a, to ^ core]).astype(jnp.int32)
        sent = call(multiply, struct((parts * rows + 8, cols), jnp.int16), [VMEM, VMEM, VMEM, SMEM])(
            mine, integrals, theirs, which
        )
        gots.append(lax.ppermute(sent, ("grp", "own"), round_pairs(r)))
    sent = call(
        lambda *refs: add_x(rows, *refs),
        struct((LOWS, (highs * units * tiles + 1) * UNIT, 128), jnp.int16),
        [VMEM] * len(gots),
    )(*gots)
    sent = call(add_low, struct((highs, (units * tiles + 1) * UNIT, 128), jnp.int16), [VMEM])(
        exchange(sent, low_groups, ("grp", "own"))
    )
    return call(add_high, struct((occ, cols), jnp.float32), [VMEM])(exchange(sent, high_groups))


def solution(mesh):
    return jax.shard_map(
        local,
        mesh=mesh,
        in_specs=(P("own", "grp", None), P("own", "grp"), P("own"), P("own")),
        out_specs=P("own", "grp"),
        check_vma=False,
    )
```

```python
import jax
import jax.numpy as jnp
from jax import lax
from jax.experimental import pallas as pl
from jax.experimental.pallas import tpu as pltpu
from jax.sharding import PartitionSpec as P

NB = 8
CAP = 2
NX = 4
UNIT = 8
CORES = 2
PAIR = 2
TOP = 32767.0
STEPS = 64.0
TINY = 1e-30
VMEM = pl.BlockSpec(memory_space=pltpu.VMEM)
SMEM = pl.BlockSpec(memory_space=pltpu.SMEM)
PARAMS = pltpu.CompilerParams(vmem_limit_bytes=40 << 20)


def code_of(largest):
    return jnp.ceil(jnp.log2(jnp.maximum(largest, TINY)) * STEPS)


def coded(values, code):
    scaled = values * (jnp.exp2(code * (-1.0 / STEPS)) * (TOP - 1.0))
    return jnp.round(scaled).astype(jnp.int32).astype(jnp.int16)


def scale_of(code16):
    code = code16.astype(jnp.int32).astype(jnp.float32)
    return jnp.exp2(code * (1.0 / STEPS)) * (1.0 / (TOP - 1.0))


def plain(values16):
    return values16.astype(jnp.int32).astype(jnp.float32)


def pack(tile_dev, amp, block, index, out, rows, blocks, tiles, keys, count, sems):
    owners, _, lanes = keys.shape
    units = rows.shape[1] // UNIT
    pairs = ((index, tiles), (block, blocks), (amp, rows))
    copies = [pltpu.make_async_copy(a, b, sems.at[n]) for n, (a, b) in enumerate(pairs)]
    for copy in copies:
        copy.start()

    def clear(o, _):
        count[o] = 0
        return 0

    lax.fori_loop(0, owners, clear, 0)
    keys[...] = jnp.full(keys.shape, -1.0, jnp.float32)
    for copy in copies:
        copy.wait()
    for r in range(rows.shape[0]):
        tile = tiles[r]
        owner = tile // tile_dev
        rank = count[owner]
        count[owner] = rank + 1
        key = blocks[r] * tile_dev + (tile - owner * tile_dev)
        for u in range(units):
            out[owner, rank * units + u] = rows[r, u * UNIT : (u + 1) * UNIT, :]
        keys[owner, pl.ds(rank, 1), :] = jnp.full((1, lanes), key, jnp.int32).astype(jnp.float32)
    for o in range(owners):
        out[o, CAP * units] = keys[o].astype(out.dtype)


def place(tile_dev, got, out, held, dense, row, key, sems):
    sources, units, _, width = got.shape
    units = (units - 1) // CAP
    line = lax.broadcasted_iota(jnp.int32, (UNIT, width), 0)
    lane = lax.broadcasted_iota(jnp.int32, (UNIT, width), 1)
    slot = jnp.where(line < CAP, lane - line, -1)
    marks = jnp.zeros((UNIT, width), jnp.float32)
    for s in range(sources):
        marks = jnp.where(slot == CAP * s, got[s, CAP * units].astype(jnp.float32), marks)
    row[...] = jnp.sum(marks, axis=0, keepdims=True).astype(jnp.int32)
    targets = out.shape[0]
    copy = pltpu.make_async_copy(row, key, sems.at[targets])
    copy.start()
    copy.wait()
    spare = NB * tile_dev
    for s in range(sources):
        for r in range(CAP):
            k = key[0, s * CAP + r]
            to = jnp.where(k < 0, spare, k)
            for u in range(units):
                held[to, u] = got[s, r * units + u]
    for b in range(NB):
        for t in range(tile_dev):
            for u in range(units):
                at = (b * units + u) * UNIT
                dense[at : at + UNIT, t * width : (t + 1) * width] = held[b * tile_dev + t, u]
    copies = [pltpu.make_async_copy(dense, out.at[y], sems.at[y]) for y in range(targets)]
    for copy in copies:
        copy.start()
    for copy in copies:
        copy.wait()


def multiply(a, mine, theirs, which, *outs):
    rows, cols = a.shape[1], outs[0].shape[1]

    def block(v, slice_at):
        p = jnp.dot(a[slice_at], v[...], preferred_element_type=jnp.float32).reshape(rows // 8, 8, cols)
        code = code_of(jnp.max(jnp.abs(p), axis=0))
        return coded(p, code[None]).reshape(rows, cols), code.astype(jnp.int32).astype(jnp.int16)

    def put(out, values, code):
        out[:rows, :] = values
        out[rows:, :] = code

    for n in range(len(outs) // CORES):
        first, second = outs[n * CORES : (n + 1) * CORES]
        for v, near in ((mine, 0), (theirs, 1)):
            values, code = block(v, which[n])

            @pl.when(which[CORES] == near)
            def _(first=first, values=values, code=code):
                put(first, values, code)

            @pl.when(which[CORES] != near)
            def _(second=second, values=values, code=code):
                put(second, values, code)


def recoded(tiles, out, z):
    largest = jnp.abs(tiles[0])
    for tile in tiles[1:]:
        largest = jnp.maximum(largest, jnp.abs(tile))
    code = code_of(largest)
    lines = code.shape[0]
    for t, tile in enumerate([*tiles, None]):
        out[z, t * lines : (t + 1) * lines, :] = (
            code.astype(jnp.int32).astype(jnp.int16) if tile is None else coded(tile, code)
        )


def decoded(got, lines):
    sources, count = got.shape[0], got.shape[1] // lines - 1
    scales = [scale_of(got[s, count * lines :, :]) for s in range(sources)]
    tiles = []
    for t in range(count):
        total = None
        for s in range(sources):
            term = plain(got[s, t * lines : (t + 1) * lines, :]) * scales[s]
            total = term if total is None else total + term
        tiles.append(total)
    return tiles


def add_x(*refs):
    *gots, out = refs
    rows, cols = gots[0].shape[0] - 8, gots[0].shape[1]
    occ = rows // NB
    scales = [scale_of(got[rows:, :]) for got in gots]
    for b in range(NB):
        tiles = []
        for u in range(occ // UNIT):
            total = None
            at = b * occ + u * UNIT
            for got, scale in zip(gots, scales):
                term = plain(got[at : at + UNIT, :]) * scale
                total = term if total is None else total + term
            tiles += [total[:, 128 * t : 128 * (t + 1)] for t in range(cols // 128)]
        recoded(tiles, out, b)


def add_z(got, out):
    lanes = out.shape[1] // 128
    for n, tile in enumerate(decoded(got, UNIT)):
        u, t = n // lanes, n % lanes
        out[u * UNIT : (u + 1) * UNIT, 128 * t : 128 * (t + 1)] = tile


def call(body, out, ins, scratch=(), place_of=VMEM):
    specs = [place_of] * len(out) if isinstance(out, list) else place_of
    return pl.pallas_call(
        body, out_shape=out, in_specs=ins, out_specs=specs, scratch_shapes=list(scratch), compiler_params=PARAMS
    )


def local(amplitudes, integrals, tile_block, tile_index):
    own, grp = lax.axis_size("own"), lax.axis_size("grp")
    nz, ny = own // NX, grp // CORES
    z_groups = [[z * NX + x for z in range(p, nz, PAIR)] for p in range(PAIR) for x in range(NX)]
    y_groups = [[y * CORES + c for y in range(ny)] for c in range(CORES)]
    core_pairs = [(y * CORES + c, y * CORES + 1 - c) for y in range(ny) for c in range(CORES)]

    def target(near, r, x, z):
        return (1 - near) ^ (x // CORES), (r // CORES) ^ (z % PAIR), (r % CORES) ^ (x % CORES)

    def round_pairs(near, r):
        pairs = []
        for g in range(grp):
            for o in range(own):
                y, c, z, x = g // CORES, g % CORES, o // NX, o % NX
                a, parity, to = target(near, r, x, z)
                if parity != z % PAIR:
                    z = (z + 1 if z % PAIR == c else z - 1) % nz
                pairs.append((g * own + o, (y * CORES + to) * own + z * NX + a * CORES + c))
        return pairs

    def exchange(array, groups=None, axis="own"):
        return lax.all_to_all(array, axis, 0, 0, axis_index_groups=groups, tiled=True)

    _, occ, width = amplitudes.shape
    units = occ // UNIT
    tile_dev = integrals.shape[0] // width
    cols = integrals.shape[1]
    rows = NB * occ
    tiles = cols // 128
    dtype = amplitudes.dtype
    struct = jax.ShapeDtypeStruct
    core = lax.axis_index("grp") % CORES
    x = lax.axis_index("own") % NX
    z = lax.axis_index("own") // NX
    anywhere = pl.BlockSpec(memory_space=pl.ANY)

    packed = call(
        lambda *refs: pack(tile_dev, *refs),
        struct((own, CAP * units + 1, UNIT, width), dtype),
        [pl.BlockSpec(memory_space=pltpu.HBM)] * 3,
        [
            pltpu.VMEM(amplitudes.shape, dtype),
            pltpu.SMEM(tile_block.shape, jnp.int32),
            pltpu.SMEM(tile_index.shape, jnp.int32),
            pltpu.VMEM((own, UNIT, width), jnp.float32),
            pltpu.SMEM((own,), jnp.int32),
            pltpu.SemaphoreType.DMA((3,)),
        ],
    )(amplitudes, tile_block, tile_index)
    theirs = lax.ppermute(integrals, "grp", core_pairs)
    copies = call(
        lambda *refs: place(tile_dev, *refs),
        struct((ny, rows, tile_dev * width), dtype),
        [VMEM],
        [
            pltpu.VMEM((NB * tile_dev + 1, units, UNIT, width), dtype),
            pltpu.VMEM((rows, tile_dev * width), dtype),
            pltpu.VMEM((1, width), jnp.int32),
            pltpu.SMEM((1, width), jnp.int32),
            pltpu.SemaphoreType.DMA((ny + 1,)),
        ],
        anywhere,
    )(exchange(packed))
    mine = exchange(copies, y_groups, "grp")
    gots = []
    for near in range(NX // CORES):
        rounds = [target(near, r, x, z) for r in range(PAIR * CORES)]
        which = [a + (NX // CORES) * parity for a, parity, _ in rounds[::CORES]] + [rounds[0][2] ^ core]
        sent = call(
            multiply, [struct((rows + 8, cols), jnp.int16)] * len(rounds), [VMEM, VMEM, VMEM, SMEM]
        )(mine, integrals, theirs, jnp.stack(which).astype(jnp.int32))
        order = sorted(range(len(rounds)), reverse=True)
        gots += [lax.ppermute(sent[r], ("grp", "own"), round_pairs(near, r)) for r in order]
    sent = call(add_x, struct((NB, (units * tiles + 1) * UNIT, 128), jnp.int16), [VMEM] * len(gots))(*gots)
    return call(add_z, struct((occ, cols), jnp.float32), [VMEM])(exchange(sent, z_groups))


def solution(mesh):
    return jax.shard_map(
        local,
        mesh=mesh,
        in_specs=(P("own", "grp", None), P("own", "grp"), P("own"), P("own")),
        out_specs=P("own", "grp"),
        check_vma=False,
    )
```

```python
import jax
import jax.numpy as jnp
from jax import lax
from jax.experimental import pallas as pl
from jax.experimental.pallas import tpu as pltpu
from jax.sharding import PartitionSpec as P

NB = 8
CAP = 2
NX = 4
UNIT = 8
CORES = 2
LOWS = 4
LINES = 2
TOP = 32767.0
STEPS = 64.0
TINY = 1e-30
VMEM = pl.BlockSpec(memory_space=pltpu.VMEM)
SMEM = pl.BlockSpec(memory_space=pltpu.SMEM)
GRANT = 40 << 20
WHOLE = 64 << 20


def code_of(largest):
    return jnp.ceil(jnp.log2(jnp.maximum(largest, TINY)) * STEPS)


def coded(values, code):
    scaled = values * (jnp.exp2(code * (-1.0 / STEPS)) * (TOP - 1.0))
    return jnp.round(scaled).astype(jnp.int32).astype(jnp.int16)


def scale_of(code16):
    code = code16.astype(jnp.int32).astype(jnp.float32)
    return jnp.exp2(code * (1.0 / STEPS)) * (1.0 / (TOP - 1.0))


def plain(values16):
    return values16.astype(jnp.int32).astype(jnp.float32)


def pack(tile_dev, amp, block, index, out, rows, blocks, tiles, keys, count, sems):
    owners, lanes = keys.shape[0] // LINES, keys.shape[1]
    units = rows.shape[1]
    pairs = ((index, tiles), (block, blocks), (amp, rows))
    copies = [pltpu.make_async_copy(a, b, sems.at[n]) for n, (a, b) in enumerate(pairs)]
    for copy in copies:
        copy.start()

    def clear(o, _):
        count[o] = 0
        return 0

    lax.fori_loop(0, owners, clear, 0)
    keys[...] = jnp.full(keys.shape, -1.0, jnp.float32)
    for copy in copies:
        copy.wait()
    for r in range(rows.shape[0]):
        tile = tiles[r]
        owner = tile // tile_dev
        rank = count[owner]
        count[owner] = rank + 1
        key = blocks[r] * tile_dev + (tile - owner * tile_dev)
        out[owner, pl.ds(rank * units, units)] = rows[r]
        line = owner * LINES + rank
        keys[pl.ds(line, 1), :] = jnp.full((1, lanes), key, jnp.int32).astype(jnp.float32)
    for o in range(owners):
        out[o, CAP * units] = keys[o * LINES : (o + 1) * LINES, :].astype(out.dtype)


def place(tile_dev, got, out, held, row, key, sems):
    sources, units, lines, width = got.shape
    units = (units - 1) // CAP
    line = lax.broadcasted_iota(jnp.int32, (lines, width), 0)
    lane = lax.broadcasted_iota(jnp.int32, (lines, width), 1)
    slot = jnp.where(line < CAP, lane - line, -1)
    marks = jnp.zeros((lines, width), jnp.float32)
    for s in range(sources):
        marks = jnp.where(slot == CAP * s, got[s, CAP * units].astype(jnp.float32), marks)
    row[...] = jnp.sum(marks, axis=0, keepdims=True).astype(jnp.int32)
    targets, keys = out.shape[0], out.shape[1]
    copy = pltpu.make_async_copy(row, key, sems.at[targets])
    copy.start()
    copy.wait()
    for s in range(sources):
        for r in range(CAP):
            k = key[0, s * CAP + r]
            held[jnp.where(k < 0, keys, k)] = got[s, r * units : (r + 1) * units]
    copies = [pltpu.make_async_copy(held.at[pl.ds(0, keys)], out.at[y], sems.at[y]) for y in range(targets)]
    for copy in copies:
        copy.start()
    for copy in copies:
        copy.wait()


def multiply(tile_dev, a, mine, theirs, which, out, left):
    rows, width, cols = NB * a.shape[2], a.shape[3], out.shape[1]
    occ = a.shape[2]
    half = NX // CORES
    parts = a.shape[0] // half
    for h in range(parts):
        for b in range(NB):
            for t in range(tile_dev):
                at = h * rows + b * occ
                left[at : at + occ, t * width : (t + 1) * width] = a[which[0] + half * h, b * tile_dev + t]

    def block(v):
        sums = [
            jnp.dot(left[h * rows : (h + 1) * rows, :], v[...], preferred_element_type=jnp.float32)
            .reshape(rows // 8, 8, cols)
            for h in range(parts)
        ]
        largest = None
        for p in sums:
            top = jnp.max(jnp.abs(p), axis=0)
            largest = top if largest is None else jnp.maximum(largest, top)
        code = code_of(largest)
        for h, p in enumerate(sums):
            out[h * rows : (h + 1) * rows, :] = coded(p, code[None]).reshape(rows, cols)
        out[len(sums) * rows :, :] = code.astype(jnp.int32).astype(jnp.int16)

    @pl.when(which[1] == 0)
    def _():
        block(mine)

    @pl.when(which[1] != 0)
    def _():
        block(theirs)


def recoded(tiles, out, z):
    largest = jnp.abs(tiles[0])
    for tile in tiles[1:]:
        largest = jnp.maximum(largest, jnp.abs(tile))
    code = code_of(largest)
    lines = code.shape[0]
    for t, tile in enumerate([*tiles, None]):
        out[z, t * lines : (t + 1) * lines, :] = (
            code.astype(jnp.int32).astype(jnp.int16) if tile is None else coded(tile, code)
        )


def decoded(got, lines):
    sources, count = got.shape[0], got.shape[1] // lines - 1
    scales = [scale_of(got[s, count * lines :, :]) for s in range(sources)]
    tiles = []
    for t in range(count):
        total = None
        for s in range(sources):
            term = plain(got[s, t * lines : (t + 1) * lines, :]) * scales[s]
            total = term if total is None else total + term
        tiles.append(total)
    return tiles


def add_x(rows, *refs):
    *gots, out = refs
    parts = (gots[0].shape[0] - 8) // rows
    cols = gots[0].shape[1]
    occ = rows // NB
    lows = out.shape[0]
    scales = [scale_of(got[parts * rows :, :]) for got in gots]
    tiles = [[] for _ in range(lows)]
    for b in range(NB):
        for h in range(parts):
            z = parts * b + h
            for u in range(occ // UNIT):
                total = None
                at = h * rows + b * occ + u * UNIT
                for got, scale in zip(gots, scales):
                    term = plain(got[at : at + UNIT, :]) * scale
                    total = term if total is None else total + term
                tiles[z % lows] += [total[:, 128 * t : 128 * (t + 1)] for t in range(cols // 128)]
    for low in range(lows):
        recoded(tiles[low], out, low)


def add_low(got, out):
    tiles = decoded(got, UNIT)
    count = len(tiles) // out.shape[0]
    for high in range(out.shape[0]):
        recoded(tiles[high * count : (high + 1) * count], out, high)


def add_high(got, out):
    lanes = out.shape[1] // 128
    for n, tile in enumerate(decoded(got, UNIT)):
        u, t = n // lanes, n % lanes
        out[u * UNIT : (u + 1) * UNIT, 128 * t : 128 * (t + 1)] = tile


def call(body, out, ins, scratch=(), place_of=VMEM, grant=GRANT):
    specs = [place_of] * len(out) if isinstance(out, list) else place_of
    return pl.pallas_call(
        body,
        out_shape=out,
        in_specs=ins,
        out_specs=specs,
        scratch_shapes=list(scratch),
        compiler_params=pltpu.CompilerParams(vmem_limit_bytes=grant),
    )


def local(amplitudes, integrals, tile_block, tile_index):
    own, grp = lax.axis_size("own"), lax.axis_size("grp")
    nz, ny = own // NX, grp // CORES
    highs = nz // LOWS
    low_groups = []
    for g in range(grp):
        shift = g % CORES * (LOWS // CORES)
        for high in range(highs):
            line = sorted(((high * LOWS + low + shift) % nz for low in range(LOWS)), key=lambda z: z % LOWS)
            low_groups += [[g * own + z * NX + x for z in line] for x in range(NX)]
    high_groups = [[(high * LOWS + low) * NX + x for high in range(highs)] for low in range(LOWS) for x in range(NX)]
    y_groups = [[y * CORES + c for y in range(ny)] for c in range(CORES)]
    core_pairs = [(y * CORES + c, y * CORES + 1 - c) for y in range(ny) for c in range(CORES)]

    def target(r, x):
        return (r // CORES) ^ (x // CORES), (r % CORES) ^ (x % CORES)

    def round_pairs(r):
        pairs = []
        for g in range(grp):
            for o in range(own):
                y, c, z, x = g // CORES, g % CORES, o // NX, o % NX
                a, to = target(r, x)
                pairs.append((g * own + o, (y * CORES + to) * own + z * NX + a * CORES + c))
        return pairs

    def exchange(array, groups=None, axis="own"):
        return lax.all_to_all(array, axis, 0, 0, axis_index_groups=groups, tiled=True)

    _, occ, width = amplitudes.shape
    units = occ // UNIT
    tile_dev = integrals.shape[0] // width
    cols = integrals.shape[1]
    rows = NB * occ
    parts = grp // NX
    tiles = cols // 128
    dtype = amplitudes.dtype
    struct = jax.ShapeDtypeStruct
    core = lax.axis_index("grp") % CORES
    x = lax.axis_index("own") % NX

    anywhere = pl.BlockSpec(memory_space=pl.ANY)
    lines = occ // LINES
    keys = NB * tile_dev
    packed = call(
        lambda *refs: pack(tile_dev, *refs),
        struct((own, CAP * lines + 1, LINES, width), dtype),
        [anywhere, anywhere, anywhere],
        [
            pltpu.VMEM((amplitudes.shape[0], lines, LINES, width), dtype),
            pltpu.SMEM(tile_block.shape, jnp.int32),
            pltpu.SMEM(tile_index.shape, jnp.int32),
            pltpu.VMEM((own * LINES, width), jnp.float32),
            pltpu.SMEM((own,), jnp.int32),
            pltpu.SemaphoreType.DMA((3,)),
        ],
        grant=WHOLE,
    )(amplitudes.reshape(-1, lines, LINES, width), tile_block, tile_index)
    theirs = lax.ppermute(integrals, "grp", core_pairs)
    copies = call(
        lambda *refs: place(tile_dev, *refs),
        struct((ny, keys, lines, LINES, width), dtype),
        [VMEM],
        [
            pltpu.VMEM((keys + 1, lines, LINES, width), dtype),
            pltpu.VMEM((1, width), jnp.int32),
            pltpu.SMEM((1, width), jnp.int32),
            pltpu.SemaphoreType.DMA((ny + 1,)),
        ],
        anywhere,
        WHOLE,
    )(exchange(packed))
    mine = exchange(copies, y_groups, "grp").reshape(ny, keys, occ, width)
    gots = []
    for r in (2, 3, 0, 1):
        a, to = target(r, x)
        which = jnp.stack([a, to ^ core]).astype(jnp.int32)
        sent = call(
            lambda *refs: multiply(tile_dev, *refs),
            struct((parts * rows + 8, cols), jnp.int16),
            [VMEM, VMEM, VMEM, SMEM],
            [pltpu.VMEM((parts * rows, tile_dev * width), dtype)],
        )(mine, integrals, theirs, which)
        gots.append(lax.ppermute(sent, ("grp", "own"), round_pairs(r)))
    sent = call(
        lambda *refs: add_x(rows, *refs),
        struct((LOWS, (highs * units * tiles + 1) * UNIT, 128), jnp.int16),
        [VMEM] * len(gots),
    )(*gots)
    sent = call(add_low, struct((highs, (units * tiles + 1) * UNIT, 128), jnp.int16), [VMEM])(
        exchange(sent, low_groups, ("grp", "own"))
    )
    return call(add_high, struct((occ, cols), jnp.float32), [VMEM])(exchange(sent, high_groups))


def solution(mesh):
    return jax.shard_map(
        local,
        mesh=mesh,
        in_specs=(P("own", "grp", None), P("own", "grp"), P("own"), P("own")),
        out_specs=P("own", "grp"),
        check_vma=False,
    )
```

```python
import jax
import jax.numpy as jnp
from jax import lax
from jax.experimental import pallas as pl
from jax.experimental.pallas import tpu as pltpu
from jax.sharding import PartitionSpec as P

NB = 8
CAP = 2
NX = 4
UNIT = 8
CORES = 2
LOWS = 4
LINES = 2
TOP = 32767.0
STEPS = 64.0
TINY = 1e-30
VMEM = pl.BlockSpec(memory_space=pltpu.VMEM)
SMEM = pl.BlockSpec(memory_space=pltpu.SMEM)
GRANT = 40 << 20
WHOLE = 64 << 20


def code_of(largest):
    return jnp.ceil(jnp.log2(jnp.maximum(largest, TINY)) * STEPS)


def coded(values, code):
    scaled = values * (jnp.exp2(code * (-1.0 / STEPS)) * (TOP - 1.0))
    return jnp.round(scaled).astype(jnp.int32).astype(jnp.int16)


def scale_of(code16):
    code = code16.astype(jnp.int32).astype(jnp.float32)
    return jnp.exp2(code * (1.0 / STEPS)) * (1.0 / (TOP - 1.0))


def plain(values16):
    return values16.astype(jnp.int32).astype(jnp.float32)


def pack(tile_dev, amp, block, index, out, rows, blocks, tiles, keys, count, sems):
    owners, lanes = keys.shape[0] // LINES, keys.shape[1]
    units = rows.shape[1]
    pairs = ((index, tiles), (block, blocks), (amp, rows))
    copies = [pltpu.make_async_copy(a, b, sems.at[n]) for n, (a, b) in enumerate(pairs)]
    for copy in copies:
        copy.start()

    def clear(o, _):
        count[o] = 0
        return 0

    lax.fori_loop(0, owners, clear, 0)
    keys[...] = jnp.full(keys.shape, -1.0, jnp.float32)
    for copy in copies[:2]:
        copy.wait()
    slots = []
    for r in range(rows.shape[0]):
        tile = tiles[r]
        owner = tile // tile_dev
        rank = count[owner]
        count[owner] = rank + 1
        key = blocks[r] * tile_dev + (tile - owner * tile_dev)
        slots.append((owner, rank))
        line = owner * LINES + rank
        keys[pl.ds(line, 1), :] = jnp.full((1, lanes), key, jnp.int32).astype(jnp.float32)
    for o in range(owners):
        out[o, CAP * units] = keys[o * LINES : (o + 1) * LINES, :].astype(out.dtype)
    copies[2].wait()
    for r, (owner, rank) in enumerate(slots):
        out[owner, pl.ds(rank * units, units)] = rows[r]


def place(tile_dev, got, out, held, row, key, slot_of, sems):
    sources, units, lines, width = got.shape
    units = (units - 1) // CAP
    line = lax.broadcasted_iota(jnp.int32, (lines, width), 0)
    lane = lax.broadcasted_iota(jnp.int32, (lines, width), 1)
    slot = jnp.where(line < CAP, lane - line, -1)
    marks = jnp.zeros((lines, width), jnp.float32)
    for s in range(sources):
        marks = jnp.where(slot == CAP * s, got[s, CAP * units].astype(jnp.float32), marks)
    row[...] = jnp.sum(marks, axis=0, keepdims=True).astype(jnp.int32)
    targets, keys = out.shape[0], out.shape[1]
    copy = pltpu.make_async_copy(row, key, sems.at[targets])
    copy.start()
    copy.wait()
    for k in range(keys):
        slot_of[k] = 0
    for n in range(sources * CAP):
        k = key[0, n]
        slot_of[jnp.where(k < 0, keys, k)] = n
    for k in range(keys):
        n = slot_of[k]
        held[k] = got[n // CAP, pl.ds(n % CAP * units, units)]
    copies = [pltpu.make_async_copy(held, out.at[y], sems.at[y]) for y in range(targets)]
    for copy in copies:
        copy.start()
    for copy in copies:
        copy.wait()


def multiply(tile_dev, a, mine, theirs, which, first, second, left):
    rows, width, cols = NB * a.shape[2], a.shape[3], first.shape[1]
    occ = a.shape[2]
    half = NX // CORES
    parts = a.shape[0] // half
    for h in range(parts):
        for b in range(NB):
            for t in range(tile_dev):
                at = h * rows + b * occ
                left[at : at + occ, t * width : (t + 1) * width] = a[which[0] + half * h, b * tile_dev + t]

    def block(v, out):
        sums = [
            jnp.dot(left[h * rows : (h + 1) * rows, :], v[...], preferred_element_type=jnp.float32)
            .reshape(rows // 8, 8, cols)
            for h in range(parts)
        ]
        largest = None
        for p in sums:
            top = jnp.max(jnp.abs(p), axis=0)
            largest = top if largest is None else jnp.maximum(largest, top)
        code = code_of(largest)
        for h, p in enumerate(sums):
            out[h * rows : (h + 1) * rows, :] = coded(p, code[None]).reshape(rows, cols)
        out[len(sums) * rows :, :] = code.astype(jnp.int32).astype(jnp.int16)

    @pl.when(which[1] == 0)
    def _():
        block(mine, first)
        block(theirs, second)

    @pl.when(which[1] != 0)
    def _():
        block(theirs, first)
        block(mine, second)


def recoded(tiles, out, z):
    largest = jnp.abs(tiles[0])
    for tile in tiles[1:]:
        largest = jnp.maximum(largest, jnp.abs(tile))
    code = code_of(largest)
    lines = code.shape[0]
    for t, tile in enumerate([*tiles, None]):
        out[z, t * lines : (t + 1) * lines, :] = (
            code.astype(jnp.int32).astype(jnp.int16) if tile is None else coded(tile, code)
        )


def decoded(got, lines):
    sources, count = got.shape[0], got.shape[1] // lines - 1
    scales = [scale_of(got[s, count * lines :, :]) for s in range(sources)]
    tiles = []
    for t in range(count):
        total = None
        for s in range(sources):
            term = plain(got[s, t * lines : (t + 1) * lines, :]) * scales[s]
            total = term if total is None else total + term
        tiles.append(total)
    return tiles


def add_x(rows, *refs):
    *gots, out = refs
    parts = (gots[0].shape[0] - 8) // rows
    cols = gots[0].shape[1]
    occ = rows // NB
    lows = out.shape[0]
    scales = [scale_of(got[parts * rows :, :]) for got in gots]
    tiles = [[] for _ in range(lows)]
    for b in range(NB):
        for h in range(parts):
            z = parts * b + h
            for u in range(occ // UNIT):
                total = None
                at = h * rows + b * occ + u * UNIT
                for got, scale in zip(gots, scales):
                    term = plain(got[at : at + UNIT, :]) * scale
                    total = term if total is None else total + term
                tiles[z % lows] += [total[:, 128 * t : 128 * (t + 1)] for t in range(cols // 128)]
    for low in range(lows):
        recoded(tiles[low], out, low)


def add_low(got, out):
    tiles = decoded(got, UNIT)
    count = len(tiles) // out.shape[0]
    for high in range(out.shape[0]):
        recoded(tiles[high * count : (high + 1) * count], out, high)


def add_high(got, out):
    lanes = out.shape[1] // 128
    for n, tile in enumerate(decoded(got, UNIT)):
        u, t = n // lanes, n % lanes
        out[u * UNIT : (u + 1) * UNIT, 128 * t : 128 * (t + 1)] = tile


def call(body, out, ins, scratch=(), place_of=VMEM, grant=GRANT):
    specs = [place_of] * len(out) if isinstance(out, list) else place_of
    return pl.pallas_call(
        body,
        out_shape=out,
        in_specs=ins,
        out_specs=specs,
        scratch_shapes=list(scratch),
        compiler_params=pltpu.CompilerParams(vmem_limit_bytes=grant),
    )


def local(amplitudes, integrals, tile_block, tile_index):
    own, grp = lax.axis_size("own"), lax.axis_size("grp")
    nz, ny = own // NX, grp // CORES
    highs = nz // LOWS
    low_groups = []
    for g in range(grp):
        shift = g % CORES * (LOWS // CORES)
        for high in range(highs):
            line = sorted(((high * LOWS + low + shift) % nz for low in range(LOWS)), key=lambda z: z % LOWS)
            low_groups += [[g * own + z * NX + x for z in line] for x in range(NX)]
    high_groups = [[(high * LOWS + low) * NX + x for high in range(highs)] for low in range(LOWS) for x in range(NX)]
    y_groups = [[y * CORES + c for y in range(ny)] for c in range(CORES)]
    core_pairs = [(y * CORES + c, y * CORES + 1 - c) for y in range(ny) for c in range(CORES)]

    def target(r, x):
        return (r // CORES) ^ (x // CORES), (r % CORES) ^ (x % CORES)

    def round_pairs(r):
        pairs = []
        for g in range(grp):
            for o in range(own):
                y, c, z, x = g // CORES, g % CORES, o // NX, o % NX
                a, to = target(r, x)
                pairs.append((g * own + o, (y * CORES + to) * own + z * NX + a * CORES + c))
        return pairs

    def exchange(array, groups=None, axis="own"):
        return lax.all_to_all(array, axis, 0, 0, axis_index_groups=groups, tiled=True)

    _, occ, width = amplitudes.shape
    units = occ // UNIT
    tile_dev = integrals.shape[0] // width
    cols = integrals.shape[1]
    rows = NB * occ
    parts = grp // NX
    tiles = cols // 128
    dtype = amplitudes.dtype
    struct = jax.ShapeDtypeStruct
    core = lax.axis_index("grp") % CORES
    x = lax.axis_index("own") % NX

    anywhere = pl.BlockSpec(memory_space=pl.ANY)
    lines = occ // LINES
    keys = NB * tile_dev
    packed = call(
        lambda *refs: pack(tile_dev, *refs),
        struct((own, CAP * lines + 1, LINES, width), dtype),
        [anywhere, anywhere, anywhere],
        [
            pltpu.VMEM((amplitudes.shape[0], lines, LINES, width), dtype),
            pltpu.SMEM(tile_block.shape, jnp.int32),
            pltpu.SMEM(tile_index.shape, jnp.int32),
            pltpu.VMEM((own * LINES, width), jnp.float32),
            pltpu.SMEM((own,), jnp.int32),
            pltpu.SemaphoreType.DMA((3,)),
        ],
        grant=WHOLE,
    )(amplitudes.reshape(-1, lines, LINES, width), tile_block, tile_index)
    theirs = lax.ppermute(integrals, "grp", core_pairs)
    copies = call(
        lambda *refs: place(tile_dev, *refs),
        struct((ny, keys, lines, LINES, width), dtype),
        [VMEM],
        [
            pltpu.VMEM((keys, lines, LINES, width), dtype),
            pltpu.VMEM((1, width), jnp.int32),
            pltpu.SMEM((1, width), jnp.int32),
            pltpu.SMEM((keys + 1,), jnp.int32),
            pltpu.SemaphoreType.DMA((ny + 1,)),
        ],
        anywhere,
        WHOLE,
    )(exchange(packed))
    mine = exchange(copies, y_groups, "grp").reshape(ny, keys, occ, width)
    gots = []
    for half in reversed(range(NX // CORES)):
        a, to = target(half * CORES, x)
        which = jnp.stack([a, to ^ core]).astype(jnp.int32)
        sent = call(
            lambda *refs: multiply(tile_dev, *refs),
            [struct((parts * rows + 8, cols), jnp.int16)] * CORES,
            [VMEM, VMEM, VMEM, SMEM],
            [pltpu.VMEM((parts * rows, tile_dev * width), dtype)],
        )(mine, integrals, theirs, which)
        gots += [lax.ppermute(sent[r], ("grp", "own"), round_pairs(half * CORES + r)) for r in range(CORES)]
    sent = call(
        lambda *refs: add_x(rows, *refs),
        struct((LOWS, (highs * units * tiles + 1) * UNIT, 128), jnp.int16),
        [VMEM] * len(gots),
    )(*gots)
    sent = call(add_low, struct((highs, (units * tiles + 1) * UNIT, 128), jnp.int16), [VMEM])(
        exchange(sent, low_groups, ("grp", "own"))
    )
    return call(add_high, struct((occ, cols), jnp.float32), [VMEM])(exchange(sent, high_groups))


def solution(mesh):
    return jax.shard_map(
        local,
        mesh=mesh,
        in_specs=(P("own", "grp", None), P("own", "grp"), P("own"), P("own")),
        out_specs=P("own", "grp"),
        check_vma=False,
    )
```

```python
import jax
import jax.numpy as jnp
from jax import lax
from jax.experimental import pallas as pl
from jax.experimental.pallas import tpu as pltpu
from jax.sharding import PartitionSpec as P

NB = 8
CAP = 2
NX = 4
UNIT = 8
CORES = 2
LOWS = 4
LINES = 2
TOP = 32767.0
STEPS = 64.0
TINY = 1e-30
VMEM = pl.BlockSpec(memory_space=pltpu.VMEM)
SMEM = pl.BlockSpec(memory_space=pltpu.SMEM)
GRANT = 40 << 20
WHOLE = 64 << 20


def code_of(largest):
    return jnp.ceil(jnp.log2(jnp.maximum(largest, TINY)) * STEPS)


def coded(values, code):
    scaled = values * (jnp.exp2(code * (-1.0 / STEPS)) * (TOP - 1.0))
    return jnp.round(scaled).astype(jnp.int32).astype(jnp.int16)


def scale_of(code16):
    code = code16.astype(jnp.int32).astype(jnp.float32)
    return jnp.exp2(code * (1.0 / STEPS)) * (1.0 / (TOP - 1.0))


def plain(values16):
    return values16.astype(jnp.int32).astype(jnp.float32)


def pack(tile_dev, amp, block, index, out, rows, blocks, tiles, keys, count, sems):
    owners, lanes = keys.shape[0] // LINES, keys.shape[1]
    units = rows.shape[1]
    pairs = ((index, tiles), (block, blocks), (amp, rows))
    copies = [pltpu.make_async_copy(a, b, sems.at[n]) for n, (a, b) in enumerate(pairs)]
    for copy in copies:
        copy.start()

    def clear(o, _):
        count[o] = 0
        return 0

    lax.fori_loop(0, owners, clear, 0)
    keys[...] = jnp.full(keys.shape, -1.0, jnp.float32)
    for copy in copies:
        copy.wait()
    for r in range(rows.shape[0]):
        tile = tiles[r]
        owner = tile // tile_dev
        rank = count[owner]
        count[owner] = rank + 1
        key = blocks[r] * tile_dev + (tile - owner * tile_dev)
        out[owner, pl.ds(rank * units, units)] = rows[r]
        line = owner * LINES + rank
        keys[pl.ds(line, 1), :] = jnp.full((1, lanes), key, jnp.int32).astype(jnp.float32)
    for o in range(owners):
        out[o, CAP * units] = keys[o * LINES : (o + 1) * LINES, :].astype(out.dtype)


def place(tile_dev, got, out, held, row, key, sems):
    sources, units, lines, width = got.shape
    units = (units - 1) // CAP
    line = lax.broadcasted_iota(jnp.int32, (lines, width), 0)
    lane = lax.broadcasted_iota(jnp.int32, (lines, width), 1)
    slot = jnp.where(line < CAP, lane - line, -1)
    marks = jnp.zeros((lines, width), jnp.float32)
    for s in range(sources):
        marks = jnp.where(slot == CAP * s, got[s, CAP * units].astype(jnp.float32), marks)
    row[...] = jnp.sum(marks, axis=0, keepdims=True).astype(jnp.int32)
    keys = out.shape[0]
    copy = pltpu.make_async_copy(row, key, sems.at[0])
    copy.start()
    copy.wait()
    for s in range(sources):
        for r in range(CAP):
            k = key[0, s * CAP + r]
            held[jnp.where(k < 0, keys, k)] = got[s, r * units : (r + 1) * units]
    copy = pltpu.make_async_copy(held.at[pl.ds(0, keys)], out, sems.at[1])
    copy.start()
    copy.wait()


def multiply(tile_dev, *refs):
    *slices, mine, theirs, which, out, left = refs
    _, occ, width = slices[0].shape
    rows, cols = NB * occ, out.shape[1]
    parts = left.shape[0] // rows
    for h in range(parts):
        for back, a in enumerate(slices):

            @pl.when(which[2 + h] == back)
            def _(h=h, a=a):
                for b in range(NB):
                    for t in range(tile_dev):
                        at = h * rows + b * occ
                        left[at : at + occ, t * width : (t + 1) * width] = a[b * tile_dev + t]

    def block(v):
        sums = [
            jnp.dot(left[h * rows : (h + 1) * rows, :], v[...], preferred_element_type=jnp.float32)
            .reshape(rows // 8, 8, cols)
            for h in range(parts)
        ]
        largest = None
        for p in sums:
            top = jnp.max(jnp.abs(p), axis=0)
            largest = top if largest is None else jnp.maximum(largest, top)
        code = code_of(largest)
        for h, p in enumerate(sums):
            out[h * rows : (h + 1) * rows, :] = coded(p, code[None]).reshape(rows, cols)
        out[len(sums) * rows :, :] = code.astype(jnp.int32).astype(jnp.int16)

    @pl.when(which[1] == 0)
    def _():
        block(mine)

    @pl.when(which[1] != 0)
    def _():
        block(theirs)


def recoded(tiles, out, z):
    largest = jnp.abs(tiles[0])
    for tile in tiles[1:]:
        largest = jnp.maximum(largest, jnp.abs(tile))
    code = code_of(largest)
    lines = code.shape[0]
    for t, tile in enumerate([*tiles, None]):
        out[z, t * lines : (t + 1) * lines, :] = (
            code.astype(jnp.int32).astype(jnp.int16) if tile is None else coded(tile, code)
        )


def decoded(got, lines):
    sources, count = got.shape[0], got.shape[1] // lines - 1
    scales = [scale_of(got[s, count * lines :, :]) for s in range(sources)]
    tiles = []
    for t in range(count):
        total = None
        for s in range(sources):
            term = plain(got[s, t * lines : (t + 1) * lines, :]) * scales[s]
            total = term if total is None else total + term
        tiles.append(total)
    return tiles


def add_x(rows, *refs):
    *gots, out = refs
    parts = (gots[0].shape[0] - 8) // rows
    cols = gots[0].shape[1]
    occ = rows // NB
    lows = out.shape[0]
    scales = [scale_of(got[parts * rows :, :]) for got in gots]
    tiles = [[] for _ in range(lows)]
    for b in range(NB):
        for h in range(parts):
            z = parts * b + h
            for u in range(occ // UNIT):
                total = None
                at = h * rows + b * occ + u * UNIT
                for got, scale in zip(gots, scales):
                    term = plain(got[at : at + UNIT, :]) * scale
                    total = term if total is None else total + term
                tiles[z % lows] += [total[:, 128 * t : 128 * (t + 1)] for t in range(cols // 128)]
    for low in range(lows):
        recoded(tiles[low], out, low)


def add_low(got, out):
    tiles = decoded(got, UNIT)
    count = len(tiles) // out.shape[0]
    for high in range(out.shape[0]):
        recoded(tiles[high * count : (high + 1) * count], out, high)


def add_high(got, out):
    lanes = out.shape[1] // 128
    for n, tile in enumerate(decoded(got, UNIT)):
        u, t = n // lanes, n % lanes
        out[u * UNIT : (u + 1) * UNIT, 128 * t : 128 * (t + 1)] = tile


def call(body, out, ins, scratch=(), place_of=VMEM, grant=GRANT):
    specs = [place_of] * len(out) if isinstance(out, list) else place_of
    return pl.pallas_call(
        body,
        out_shape=out,
        in_specs=ins,
        out_specs=specs,
        scratch_shapes=list(scratch),
        compiler_params=pltpu.CompilerParams(vmem_limit_bytes=grant),
    )


def local(amplitudes, integrals, tile_block, tile_index):
    own, grp = lax.axis_size("own"), lax.axis_size("grp")
    nz, ny = own // NX, grp // CORES
    highs = nz // LOWS
    low_groups = []
    for g in range(grp):
        shift = g % CORES * (LOWS // CORES)
        for high in range(highs):
            line = sorted(((high * LOWS + low + shift) % nz for low in range(LOWS)), key=lambda z: z % LOWS)
            low_groups += [[g * own + z * NX + x for z in line] for x in range(NX)]
    high_groups = [[(high * LOWS + low) * NX + x for high in range(highs)] for low in range(LOWS) for x in range(NX)]
    core_pairs = [(y * CORES + c, y * CORES + 1 - c) for y in range(ny) for c in range(CORES)]

    def target(r, x):
        return (r // CORES) ^ (x // CORES), (r % CORES) ^ (x % CORES)

    def round_pairs(r):
        pairs = []
        for g in range(grp):
            for o in range(own):
                y, c, z, x = g // CORES, g % CORES, o // NX, o % NX
                a, to = target(r, x)
                pairs.append((g * own + o, (y * CORES + to) * own + z * NX + a * CORES + c))
        return pairs

    def y_pairs(k):
        return [(g, (g + k * CORES) % grp) for g in range(grp)]

    def exchange(array, groups=None, axis="own"):
        return lax.all_to_all(array, axis, 0, 0, axis_index_groups=groups, tiled=True)

    _, occ, width = amplitudes.shape
    units = occ // UNIT
    tile_dev = integrals.shape[0] // width
    cols = integrals.shape[1]
    rows = NB * occ
    parts = grp // NX
    tiles = cols // 128
    dtype = amplitudes.dtype
    struct = jax.ShapeDtypeStruct
    core = lax.axis_index("grp") % CORES
    y = lax.axis_index("grp") // CORES
    x = lax.axis_index("own") % NX

    anywhere = pl.BlockSpec(memory_space=pl.ANY)
    lines = occ // LINES
    keys = NB * tile_dev
    packed = call(
        lambda *refs: pack(tile_dev, *refs),
        struct((own, CAP * lines + 1, LINES, width), dtype),
        [anywhere, anywhere, anywhere],
        [
            pltpu.VMEM((amplitudes.shape[0], lines, LINES, width), dtype),
            pltpu.SMEM(tile_block.shape, jnp.int32),
            pltpu.SMEM(tile_index.shape, jnp.int32),
            pltpu.VMEM((own * LINES, width), jnp.float32),
            pltpu.SMEM((own,), jnp.int32),
            pltpu.SemaphoreType.DMA((3,)),
        ],
        grant=WHOLE,
    )(amplitudes.reshape(-1, lines, LINES, width), tile_block, tile_index)
    theirs = lax.ppermute(integrals, "grp", core_pairs)
    placed = call(
        lambda *refs: place(tile_dev, *refs),
        struct((keys, lines, LINES, width), dtype),
        [VMEM],
        [
            pltpu.VMEM((keys + 1, lines, LINES, width), dtype),
            pltpu.VMEM((1, width), jnp.int32),
            pltpu.SMEM((1, width), jnp.int32),
            pltpu.SemaphoreType.DMA((2,)),
        ],
        anywhere,
        WHOLE,
    )(exchange(packed))
    far_first = sorted(range(1, ny), key=lambda k: k % CORES)
    slices = {k: lax.ppermute(placed, "grp", y_pairs(k)) for k in far_first}
    slices = [s.reshape(keys, occ, width) for s in (placed, *(slices[k] for k in range(1, ny)))]
    gots = []
    for r in (2, 3, 0, 1):
        a, to = target(r, x)
        back = [(y - a - NX // CORES * h) % ny for h in range(parts)]
        which = jnp.stack([a, to ^ core, *back]).astype(jnp.int32)
        sent = call(
            lambda *refs: multiply(tile_dev, *refs),
            struct((parts * rows + 8, cols), jnp.int16),
            [VMEM] * (ny + 2) + [SMEM],
            [pltpu.VMEM((parts * rows, tile_dev * width), dtype)],
        )(*slices, integrals, theirs, which)
        gots.append(lax.ppermute(sent, ("grp", "own"), round_pairs(r)))
    sent = call(
        lambda *refs: add_x(rows, *refs),
        struct((LOWS, (highs * units * tiles + 1) * UNIT, 128), jnp.int16),
        [VMEM] * len(gots),
    )(*gots)
    sent = call(add_low, struct((highs, (units * tiles + 1) * UNIT, 128), jnp.int16), [VMEM])(
        exchange(sent, low_groups, ("grp", "own"))
    )
    return call(add_high, struct((occ, cols), jnp.float32), [VMEM])(exchange(sent, high_groups))


def solution(mesh):
    return jax.shard_map(
        local,
        mesh=mesh,
        in_specs=(P("own", "grp", None), P("own", "grp"), P("own"), P("own")),
        out_specs=P("own", "grp"),
        check_vma=False,
    )
```

```python
import jax
import jax.numpy as jnp
from jax import lax
from jax.experimental import pallas as pl
from jax.experimental.pallas import tpu as pltpu
from jax.sharding import PartitionSpec as P

NB = 8
CAP = 2
NX = 4
UNIT = 8
CORES = 2
PAIR = 2
LINES = 2
TOP = 32767.0
STEPS = 64.0
TINY = 1e-30
VMEM = pl.BlockSpec(memory_space=pltpu.VMEM)
SMEM = pl.BlockSpec(memory_space=pltpu.SMEM)
GRANT = 40 << 20
WHOLE = 64 << 20


def code_of(largest):
    return jnp.ceil(jnp.log2(jnp.maximum(largest, TINY)) * STEPS)


def coded(values, code):
    scaled = values * (jnp.exp2(code * (-1.0 / STEPS)) * (TOP - 1.0))
    return jnp.round(scaled).astype(jnp.int32).astype(jnp.int16)


def scale_of(code16):
    code = code16.astype(jnp.int32).astype(jnp.float32)
    return jnp.exp2(code * (1.0 / STEPS)) * (1.0 / (TOP - 1.0))


def plain(values16):
    return values16.astype(jnp.int32).astype(jnp.float32)


def pack(tile_dev, amp, block, index, out, rows, blocks, tiles, keys, count, sems):
    owners, lanes = keys.shape[0] // LINES, keys.shape[1]
    units = rows.shape[1]
    pairs = ((index, tiles), (block, blocks), (amp, rows))
    copies = [pltpu.make_async_copy(a, b, sems.at[n]) for n, (a, b) in enumerate(pairs)]
    for copy in copies:
        copy.start()

    def clear(o, _):
        count[o] = 0
        return 0

    lax.fori_loop(0, owners, clear, 0)
    keys[...] = jnp.full(keys.shape, -1.0, jnp.float32)
    for copy in copies:
        copy.wait()
    for r in range(rows.shape[0]):
        tile = tiles[r]
        owner = tile // tile_dev
        rank = count[owner]
        count[owner] = rank + 1
        key = blocks[r] * tile_dev + (tile - owner * tile_dev)
        out[owner, pl.ds(rank * units, units)] = rows[r]
        line = owner * LINES + rank
        keys[pl.ds(line, 1), :] = jnp.full((1, lanes), key, jnp.int32).astype(jnp.float32)
    for o in range(owners):
        out[o, CAP * units] = keys[o * LINES : (o + 1) * LINES, :].astype(out.dtype)


def place(tile_dev, got, out, held, row, key, sems):
    sources, units, lines, width = got.shape
    units = (units - 1) // CAP
    line = lax.broadcasted_iota(jnp.int32, (lines, width), 0)
    lane = lax.broadcasted_iota(jnp.int32, (lines, width), 1)
    slot = jnp.where(line < CAP, lane - line, -1)
    marks = jnp.zeros((lines, width), jnp.float32)
    for s in range(sources):
        marks = jnp.where(slot == CAP * s, got[s, CAP * units].astype(jnp.float32), marks)
    row[...] = jnp.sum(marks, axis=0, keepdims=True).astype(jnp.int32)
    targets, keys = out.shape[0], out.shape[1]
    copy = pltpu.make_async_copy(row, key, sems.at[targets])
    copy.start()
    copy.wait()
    for s in range(sources):
        for r in range(CAP):
            k = key[0, s * CAP + r]
            held[jnp.where(k < 0, keys, k)] = got[s, r * units : (r + 1) * units]
    copies = [pltpu.make_async_copy(held.at[pl.ds(0, keys)], out.at[y], sems.at[y]) for y in range(targets)]
    for copy in copies:
        copy.start()
    for copy in copies:
        copy.wait()


def multiply(tile_dev, a, mine, theirs, which, out, left):
    rows, width, cols = NB * a.shape[2], a.shape[3], out.shape[1]
    occ = a.shape[2]
    half = NX // CORES
    parts = a.shape[0] // half
    for h in range(parts):
        for b in range(NB):
            for t in range(tile_dev):
                at = h * rows + b * occ
                left[at : at + occ, t * width : (t + 1) * width] = a[which[0] + half * h, b * tile_dev + t]

    def block(v):
        sums = [
            jnp.dot(left[h * rows : (h + 1) * rows, :], v[...], preferred_element_type=jnp.float32)
            .reshape(rows // 8, 8, cols)
            for h in range(parts)
        ]
        largest = None
        for p in sums:
            top = jnp.max(jnp.abs(p), axis=0)
            largest = top if largest is None else jnp.maximum(largest, top)
        code = code_of(largest)
        for h, p in enumerate(sums):
            out[h * rows : (h + 1) * rows, :] = coded(p, code[None]).reshape(rows, cols)
        out[len(sums) * rows :, :] = code.astype(jnp.int32).astype(jnp.int16)

    @pl.when(which[1] == 0)
    def _():
        block(mine)

    @pl.when(which[1] != 0)
    def _():
        block(theirs)


def recoded(tiles, out, z):
    largest = jnp.abs(tiles[0])
    for tile in tiles[1:]:
        largest = jnp.maximum(largest, jnp.abs(tile))
    code = code_of(largest)
    lines = code.shape[0]
    for t, tile in enumerate([*tiles, None]):
        out[z, t * lines : (t + 1) * lines, :] = (
            code.astype(jnp.int32).astype(jnp.int16) if tile is None else coded(tile, code)
        )


def decoded(got, lines):
    sources, count = got.shape[0], got.shape[1] // lines - 1
    scales = [scale_of(got[s, count * lines :, :]) for s in range(sources)]
    tiles = []
    for t in range(count):
        total = None
        for s in range(sources):
            term = plain(got[s, t * lines : (t + 1) * lines, :]) * scales[s]
            total = term if total is None else total + term
        tiles.append(total)
    return tiles


def add_x(which, *refs):
    *gots, kept, out, held = refs
    parts, blocks = held.shape[0], held.shape[1]
    rows = (gots[0].shape[0] - 8) // parts
    cols = gots[0].shape[1]
    occ = rows // blocks
    lanes = cols // 128
    scales = [scale_of(got[parts * rows :, :]) for got in gots]
    for h in range(parts):
        for b in range(blocks):
            for u in range(occ // UNIT):
                total = None
                at = h * rows + b * occ + u * UNIT
                for got, scale in zip(gots, scales):
                    term = plain(got[at : at + UNIT, :]) * scale
                    total = term if total is None else total + term
                for t in range(lanes):
                    held[h, b, u * lanes + t] = total[:, 128 * t : 128 * (t + 1)]
    other = 1 - which[0]
    for b in range(blocks):
        recoded([held[other, b, n] for n in range(held.shape[2])], out, b)
    kept[...] = held[which[0]]


def add_pair(kept, got, out):
    count = kept.shape[1]
    for b in range(kept.shape[0]):
        scale = scale_of(got[b, count * UNIT :, :])
        recoded([kept[b, n] + plain(got[b, n * UNIT : (n + 1) * UNIT, :]) * scale for n in range(count)], out, b)


def add_z(got, out):
    lanes = out.shape[1] // 128
    for n, tile in enumerate(decoded(got, UNIT)):
        u, t = n // lanes, n % lanes
        out[u * UNIT : (u + 1) * UNIT, 128 * t : 128 * (t + 1)] = tile


def call(body, out, ins, scratch=(), place_of=VMEM, grant=GRANT):
    specs = [place_of] * len(out) if isinstance(out, list) else place_of
    return pl.pallas_call(
        body,
        out_shape=out,
        in_specs=ins,
        out_specs=specs,
        scratch_shapes=list(scratch),
        compiler_params=pltpu.CompilerParams(vmem_limit_bytes=grant),
    )


def local(amplitudes, integrals, tile_block, tile_index):
    own, grp = lax.axis_size("own"), lax.axis_size("grp")
    nz, ny = own // NX, grp // CORES
    z_groups = [[z * NX + x for z in range(p, nz, PAIR)] for p in range(PAIR) for x in range(NX)]
    z_pairs = []
    for g in range(grp):
        for o in range(own):
            z = o // NX
            partner = (z + 1 if z % PAIR == g % CORES else z - 1) % nz
            z_pairs.append((g * own + o, g * own + partner * NX + o % NX))
    y_groups = [[y * CORES + c for y in range(ny)] for c in range(CORES)]
    core_pairs = [(y * CORES + c, y * CORES + 1 - c) for y in range(ny) for c in range(CORES)]

    def target(r, x):
        return (r // CORES) ^ (x // CORES), (r % CORES) ^ (x % CORES)

    def round_pairs(r):
        pairs = []
        for g in range(grp):
            for o in range(own):
                y, c, z, x = g // CORES, g % CORES, o // NX, o % NX
                a, to = target(r, x)
                pairs.append((g * own + o, (y * CORES + to) * own + z * NX + a * CORES + c))
        return pairs

    def exchange(array, groups=None, axis="own"):
        return lax.all_to_all(array, axis, 0, 0, axis_index_groups=groups, tiled=True)

    _, occ, width = amplitudes.shape
    units = occ // UNIT
    tile_dev = integrals.shape[0] // width
    cols = integrals.shape[1]
    rows = NB * occ
    parts = grp // NX
    tiles = cols // 128
    dtype = amplitudes.dtype
    struct = jax.ShapeDtypeStruct
    core = lax.axis_index("grp") % CORES
    x = lax.axis_index("own") % NX

    anywhere = pl.BlockSpec(memory_space=pl.ANY)
    lines = occ // LINES
    keys = NB * tile_dev
    packed = call(
        lambda *refs: pack(tile_dev, *refs),
        struct((own, CAP * lines + 1, LINES, width), dtype),
        [anywhere, anywhere, anywhere],
        [
            pltpu.VMEM((amplitudes.shape[0], lines, LINES, width), dtype),
            pltpu.SMEM(tile_block.shape, jnp.int32),
            pltpu.SMEM(tile_index.shape, jnp.int32),
            pltpu.VMEM((own * LINES, width), jnp.float32),
            pltpu.SMEM((own,), jnp.int32),
            pltpu.SemaphoreType.DMA((3,)),
        ],
        grant=WHOLE,
    )(amplitudes.reshape(-1, lines, LINES, width), tile_block, tile_index)
    theirs = lax.ppermute(integrals, "grp", core_pairs)
    copies = call(
        lambda *refs: place(tile_dev, *refs),
        struct((ny, keys, lines, LINES, width), dtype),
        [VMEM],
        [
            pltpu.VMEM((keys + 1, lines, LINES, width), dtype),
            pltpu.VMEM((1, width), jnp.int32),
            pltpu.SMEM((1, width), jnp.int32),
            pltpu.SemaphoreType.DMA((ny + 1,)),
        ],
        anywhere,
        WHOLE,
    )(exchange(packed))
    mine = exchange(copies, y_groups, "grp").reshape(ny, keys, occ, width)
    gots = []
    for r in (2, 3, 0, 1):
        a, to = target(r, x)
        which = jnp.stack([a, to ^ core]).astype(jnp.int32)
        sent = call(
            lambda *refs: multiply(tile_dev, *refs),
            struct((parts * rows + 8, cols), jnp.int16),
            [VMEM, VMEM, VMEM, SMEM],
            [pltpu.VMEM((parts * rows, tile_dev * width), dtype)],
        )(mine, integrals, theirs, which)
        gots.append(lax.ppermute(sent, ("grp", "own"), round_pairs(r)))
    parity = jnp.reshape(lax.axis_index("own") // NX % PAIR, (1,)).astype(jnp.int32)
    count = units * tiles
    coded_sums = struct((NB, (count + 1) * UNIT, 128), jnp.int16)
    kept, sent = call(
        add_x,
        [struct((NB, count, UNIT, 128), jnp.float32), coded_sums],
        [SMEM] + [VMEM] * len(gots),
        [pltpu.VMEM((PAIR, NB, count, UNIT, 128), jnp.float32)],
    )(parity, *gots)
    sent = call(add_pair, coded_sums, [VMEM, VMEM])(kept, lax.ppermute(sent, ("grp", "own"), z_pairs))
    return call(add_z, struct((occ, cols), jnp.float32), [VMEM])(exchange(sent, z_groups))


def solution(mesh):
    return jax.shard_map(
        local,
        mesh=mesh,
        in_specs=(P("own", "grp", None), P("own", "grp"), P("own"), P("own")),
        out_specs=P("own", "grp"),
        check_vma=False,
    )
```

```python
import jax
import jax.numpy as jnp
from jax import lax
from jax.experimental import pallas as pl
from jax.experimental.pallas import tpu as pltpu
from jax.sharding import PartitionSpec as P

NB = 8
CAP = 2
NX = 4
UNIT = 8
CORES = 2
PAIR = 2
LINES = 2
TOP = 32767.0
STEPS = 64.0
TINY = 1e-30
VMEM = pl.BlockSpec(memory_space=pltpu.VMEM)
SMEM = pl.BlockSpec(memory_space=pltpu.SMEM)
GRANT = 40 << 20
WHOLE = 64 << 20


def code_of(largest):
    return jnp.ceil(jnp.log2(jnp.maximum(largest, TINY)) * STEPS)


def coded(values, code):
    scaled = values * (jnp.exp2(code * (-1.0 / STEPS)) * (TOP - 1.0))
    return jnp.round(scaled).astype(jnp.int32).astype(jnp.int16)


def scale_of(code16):
    code = code16.astype(jnp.int32).astype(jnp.float32)
    return jnp.exp2(code * (1.0 / STEPS)) * (1.0 / (TOP - 1.0))


def plain(values16):
    return values16.astype(jnp.int32).astype(jnp.float32)


def pack(tile_dev, amp, block, index, out, rows, blocks, tiles, keys, count, sems):
    owners, lanes = keys.shape[0] // LINES, keys.shape[1]
    units = rows.shape[1]
    pairs = ((index, tiles), (block, blocks), (amp, rows))
    copies = [pltpu.make_async_copy(a, b, sems.at[n]) for n, (a, b) in enumerate(pairs)]
    for copy in copies:
        copy.start()

    def clear(o, _):
        count[o] = 0
        return 0

    lax.fori_loop(0, owners, clear, 0)
    keys[...] = jnp.full(keys.shape, -1.0, jnp.float32)
    for copy in copies:
        copy.wait()
    for r in range(rows.shape[0]):
        tile = tiles[r]
        owner = tile // tile_dev
        rank = count[owner]
        count[owner] = rank + 1
        key = blocks[r] * tile_dev + (tile - owner * tile_dev)
        out[owner, pl.ds(rank * units, units)] = rows[r]
        line = owner * LINES + rank
        keys[pl.ds(line, 1), :] = jnp.full((1, lanes), key, jnp.int32).astype(jnp.float32)
    for o in range(owners):
        out[o, CAP * units] = keys[o * LINES : (o + 1) * LINES, :].astype(out.dtype)


def place(tile_dev, got, out, held, row, key, sems):
    sources, units, lines, width = got.shape
    units = (units - 1) // CAP
    line = lax.broadcasted_iota(jnp.int32, (lines, width), 0)
    lane = lax.broadcasted_iota(jnp.int32, (lines, width), 1)
    slot = jnp.where(line < CAP, lane - line, -1)
    marks = jnp.zeros((lines, width), jnp.float32)
    for s in range(sources):
        marks = jnp.where(slot == CAP * s, got[s, CAP * units].astype(jnp.float32), marks)
    row[...] = jnp.sum(marks, axis=0, keepdims=True).astype(jnp.int32)
    targets, keys = out.shape[0], out.shape[1]
    copy = pltpu.make_async_copy(row, key, sems.at[targets])
    copy.start()
    copy.wait()
    for s in range(sources):
        for r in range(CAP):
            k = key[0, s * CAP + r]
            held[jnp.where(k < 0, keys, k)] = got[s, r * units : (r + 1) * units]
    copies = [pltpu.make_async_copy(held.at[pl.ds(0, keys)], out.at[y], sems.at[y]) for y in range(targets)]
    for copy in copies:
        copy.start()
    for copy in copies:
        copy.wait()


def multiply(tile_dev, a, mine, theirs, which, out, left):
    rows, width, cols = NB * a.shape[2], a.shape[3], out.shape[1]
    occ = a.shape[2]
    half = NX // CORES
    parts = a.shape[0] // half
    for h in range(parts):
        for b in range(NB):
            for t in range(tile_dev):
                at = h * rows + b * occ
                left[at : at + occ, t * width : (t + 1) * width] = a[which[0] + half * h, b * tile_dev + t]

    def block(v):
        sums = [
            jnp.dot(left[h * rows : (h + 1) * rows, :], v[...], preferred_element_type=jnp.float32)
            .reshape(rows // 8, 8, cols)
            for h in range(parts)
        ]
        largest = None
        for p in sums:
            top = jnp.max(jnp.abs(p), axis=0)
            largest = top if largest is None else jnp.maximum(largest, top)
        code = code_of(largest)
        for h, p in enumerate(sums):
            out[h * rows : (h + 1) * rows, :] = coded(p, code[None]).reshape(rows, cols)
        out[len(sums) * rows :, :] = code.astype(jnp.int32).astype(jnp.int16)

    @pl.when(which[1] == 0)
    def _():
        block(mine)

    @pl.when(which[1] != 0)
    def _():
        block(theirs)


def recoded(tiles, out, z):
    largest = jnp.abs(tiles[0])
    for tile in tiles[1:]:
        largest = jnp.maximum(largest, jnp.abs(tile))
    code = code_of(largest)
    lines = code.shape[0]
    for t, tile in enumerate([*tiles, None]):
        out[z, t * lines : (t + 1) * lines, :] = (
            code.astype(jnp.int32).astype(jnp.int16) if tile is None else coded(tile, code)
        )


def decoded(got, lines):
    sources, count = got.shape[0], got.shape[1] // lines - 1
    scales = [scale_of(got[s, count * lines :, :]) for s in range(sources)]
    tiles = []
    for t in range(count):
        total = None
        for s in range(sources):
            term = plain(got[s, t * lines : (t + 1) * lines, :]) * scales[s]
            total = term if total is None else total + term
        tiles.append(total)
    return tiles


def add_x(which, *refs):
    *gots, kept, out = refs
    blocks = kept.shape[0]
    rows = (gots[0].shape[0] - 8) // PAIR
    cols = gots[0].shape[1]
    occ = rows // blocks
    scales = [scale_of(got[PAIR * rows :, :]) for got in gots]

    def tiles_of(h, b):
        tiles = []
        for u in range(occ // UNIT):
            total = None
            at = h * rows + b * occ + u * UNIT
            for got, scale in zip(gots, scales):
                term = plain(got[at : at + UNIT, :]) * scale
                total = term if total is None else total + term
            tiles += [total[:, 128 * t : 128 * (t + 1)] for t in range(cols // 128)]
        return tiles

    for parity in range(PAIR):

        @pl.when(which[0] == parity)
        def _(parity=parity):
            for b in range(blocks):
                recoded(tiles_of(1 - parity, b), out, b)
                for n, tile in enumerate(tiles_of(parity, b)):
                    kept[b, n] = tile


def add_pair(kept, got, out):
    count = kept.shape[1]
    for b in range(kept.shape[0]):
        scale = scale_of(got[b, count * UNIT :, :])
        recoded([kept[b, n] + plain(got[b, n * UNIT : (n + 1) * UNIT, :]) * scale for n in range(count)], out, b)


def add_z(got, out):
    lanes = out.shape[1] // 128
    for n, tile in enumerate(decoded(got, UNIT)):
        u, t = n // lanes, n % lanes
        out[u * UNIT : (u + 1) * UNIT, 128 * t : 128 * (t + 1)] = tile


def call(body, out, ins, scratch=(), place_of=VMEM, grant=GRANT):
    specs = [place_of] * len(out) if isinstance(out, list) else place_of
    return pl.pallas_call(
        body,
        out_shape=out,
        in_specs=ins,
        out_specs=specs,
        scratch_shapes=list(scratch),
        compiler_params=pltpu.CompilerParams(vmem_limit_bytes=grant),
    )


def local(amplitudes, integrals, tile_block, tile_index):
    own, grp = lax.axis_size("own"), lax.axis_size("grp")
    nz, ny = own // NX, grp // CORES
    z_groups = [[z * NX + x for z in range(p, nz, PAIR)] for p in range(PAIR) for x in range(NX)]
    z_pairs = []
    for g in range(grp):
        for o in range(own):
            z = o // NX
            partner = (z + 1 if z % PAIR == g % CORES else z - 1) % nz
            z_pairs.append((g * own + o, g * own + partner * NX + o % NX))
    y_groups = [[y * CORES + c for y in range(ny)] for c in range(CORES)]
    core_pairs = [(y * CORES + c, y * CORES + 1 - c) for y in range(ny) for c in range(CORES)]

    def target(r, x):
        return (r // CORES) ^ (x // CORES), (r % CORES) ^ (x % CORES)

    def round_pairs(r):
        pairs = []
        for g in range(grp):
            for o in range(own):
                y, c, z, x = g // CORES, g % CORES, o // NX, o % NX
                a, to = target(r, x)
                pairs.append((g * own + o, (y * CORES + to) * own + z * NX + a * CORES + c))
        return pairs

    def exchange(array, groups=None, axis="own"):
        return lax.all_to_all(array, axis, 0, 0, axis_index_groups=groups, tiled=True)

    _, occ, width = amplitudes.shape
    units = occ // UNIT
    tile_dev = integrals.shape[0] // width
    cols = integrals.shape[1]
    rows = NB * occ
    parts = grp // NX
    tiles = cols // 128
    dtype = amplitudes.dtype
    struct = jax.ShapeDtypeStruct
    core = lax.axis_index("grp") % CORES
    x = lax.axis_index("own") % NX

    anywhere = pl.BlockSpec(memory_space=pl.ANY)
    lines = occ // LINES
    keys = NB * tile_dev
    packed = call(
        lambda *refs: pack(tile_dev, *refs),
        struct((own, CAP * lines + 1, LINES, width), dtype),
        [anywhere, anywhere, anywhere],
        [
            pltpu.VMEM((amplitudes.shape[0], lines, LINES, width), dtype),
            pltpu.SMEM(tile_block.shape, jnp.int32),
            pltpu.SMEM(tile_index.shape, jnp.int32),
            pltpu.VMEM((own * LINES, width), jnp.float32),
            pltpu.SMEM((own,), jnp.int32),
            pltpu.SemaphoreType.DMA((3,)),
        ],
        grant=WHOLE,
    )(amplitudes.reshape(-1, lines, LINES, width), tile_block, tile_index)
    theirs = lax.ppermute(integrals, "grp", core_pairs)
    copies = call(
        lambda *refs: place(tile_dev, *refs),
        struct((ny, keys, lines, LINES, width), dtype),
        [VMEM],
        [
            pltpu.VMEM((keys + 1, lines, LINES, width), dtype),
            pltpu.VMEM((1, width), jnp.int32),
            pltpu.SMEM((1, width), jnp.int32),
            pltpu.SemaphoreType.DMA((ny + 1,)),
        ],
        anywhere,
        WHOLE,
    )(exchange(packed))
    mine = exchange(copies, y_groups, "grp").reshape(ny, keys, occ, width)
    gots = []
    for r in (2, 3, 0, 1):
        a, to = target(r, x)
        which = jnp.stack([a, to ^ core]).astype(jnp.int32)
        sent = call(
            lambda *refs: multiply(tile_dev, *refs),
            struct((parts * rows + 8, cols), jnp.int16),
            [VMEM, VMEM, VMEM, SMEM],
            [pltpu.VMEM((parts * rows, tile_dev * width), dtype)],
        )(mine, integrals, theirs, which)
        gots.append(lax.ppermute(sent, ("grp", "own"), round_pairs(r)))
    parity = jnp.reshape(lax.axis_index("own") // NX % PAIR, (1,)).astype(jnp.int32)
    count = units * tiles
    coded_sums = struct((NB, (count + 1) * UNIT, 128), jnp.int16)
    kept, sent = call(
        add_x,
        [struct((NB, count, UNIT, 128), jnp.float32), coded_sums],
        [SMEM] + [VMEM] * len(gots),
    )(parity, *gots)
    sent = call(add_pair, coded_sums, [VMEM, VMEM])(kept, lax.ppermute(sent, ("grp", "own"), z_pairs))
    return call(add_z, struct((occ, cols), jnp.float32), [VMEM])(exchange(sent, z_groups))


def solution(mesh):
    return jax.shard_map(
        local,
        mesh=mesh,
        in_specs=(P("own", "grp", None), P("own", "grp"), P("own"), P("own")),
        out_specs=P("own", "grp"),
        check_vma=False,
    )
```
